256 devices in a mesh: sec: 16 (over y_lo, x, core), tile: 16 (over y_hi, z).
Axes of the slice: x: 4, y: 4 (y_hi: 2, y_lo: 2; y = y_hi * 2 + y_lo), z: 8, core: 2. Of those that a mesh axis runs over, the one named last changes fastest.
Arguments:
- displacement: float32 [2, 32, 128, 2048], P(None, 'sec', 'tile'), may hold values from -6 to 6
- velocity: float32 [2, 32, 128, 2048], P(None, 'sec', 'tile'), may hold values from -10 to 10
- frac: bfloat16 [2, 4, 32, 128, 2048], P(None, None, 'sec', 'tile'), may hold values from 0 to 1
- offsets: int32 [4, 32, 16, 2], P(None, 'sec', 'tile'), may hold values from -2 to 2
- fixed: int32 [32, 128, 2048], P('sec', 'tile'), may hold values 0 or 1
- trans: float32 [32, 2], P('sec'), may hold values from -0.3 to 0.3
Outputs:
- new_displacement: float32 [2, 32, 128, 2048], P(None, 'sec', 'tile')
- new_velocity: float32 [2, 32, 128, 2048], P(None, 'sec', 'tile')
The draws below stay inside these ranges and needn't reach their ends.
All inputs are finite; a program needn't handle non-finite values. No bound on the sum of `fixed` on one device may be relied on, other than what follows from the above.
Results may differ from the reference program's by a relative error of at most 0.0003.
Values sent between devices are 32-bit elements; how exact they have to be, the bound alone decides.
No kernel may reach another device: no remote copies, remote signals or barrier semaphores. Data moves between devices by JAX's collectives and lax.ppermute only.
A program may use at most 64 MiB of HBM per device.

```python
import jax
import jax.numpy as jnp
from jax import lax

TR = 8
COLS = 2048
ITERS = 3
SECTIONS = 32
TILES = 16
ROWS = 128


def draw_velocity(key, part):
    sec_scale = 0.4 + 1.2 * jnp.arange(SECTIONS, dtype=jnp.float32) / SECTIONS
    row_scale = 0.5 + jnp.arange(ROWS, dtype=jnp.float32) / ROWS
    scale = sec_scale[:, None, None] * row_scale[None, :, None]
    base = jnp.clip(jax.random.normal(key, (2, SECTIONS, ROWS, COLS), jnp.float32), -4.0, 4.0)
    return base * scale[None]


def place_ends(entries, rng, least, top_value):
    spot = [jax.random.randint(jax.random.fold_in(rng, axis), (), 0, length) for axis, length in enumerate(entries.shape)]
    longest = entries.shape.index(max(entries.shape))
    beside = spot[:longest] + [(spot[longest] + 1) % entries.shape[longest]] + spot[longest + 1:]
    return entries.at[tuple(spot)].set(least).at[tuple(beside)].set(top_value)


def levels(rng, shape, pieces, low, high):
    def one(position, shards_of):
        heights = jax.random.uniform(jax.random.fold_in(jax.random.fold_in(rng, 6), position), (shards_of,), jnp.float32, low / len(pieces), high / len(pieces))
        return jnp.repeat(jnp.exp(heights), shape[position] // shards_of).reshape((-1,) + (1,) * (len(shape) - position - 1))

    factor_of = one(*pieces[0])
    for cut in pieces[1:]:
        factor_of = factor_of * one(*cut)
    return factor_of


def bell_draw(own_key, extent, scale, limit, split=(), kind=jnp.bfloat16):
    result = jax.random.normal(own_key, extent, jnp.float32) * scale
    if len(split) > 0:
        result = levels(own_key, extent, split, -0.22, 0.18) * result
    return jnp.clip(result, min=-limit, max=limit).astype(kind)


def setup_inputs(seed: int = 0) -> dict:
    streams_of = jax.random.split(jax.random.key(seed), 7)
    return {
        "displacement": bell_draw(streams_of[0], (2, SECTIONS, ROWS, COLS), 1.0, 6.0, ((1, 16), (2, 16)), jnp.float32),
        "velocity": draw_velocity(jax.random.fold_in(streams_of[6], 71), 0),
        "frac": jnp.clip(1.0 * jax.random.uniform(streams_of[2], (2, 4, SECTIONS, ROWS, COLS), jnp.float32) ** levels(streams_of[2], (2, 4, SECTIONS, ROWS, COLS), ((2, 16), (3, 16)), -0.2, 0.2), 0.0, 1.0).astype(jnp.bfloat16),
        "offsets": place_ends(jax.random.randint(streams_of[3], (4, SECTIONS, TILES, 2), -2, 3), jax.random.fold_in(streams_of[3], 1), -2, 2).astype(jnp.int32),
        "fixed": place_ends((jax.random.randint(streams_of[4], (SECTIONS, ROWS, COLS), 0, 16) < 1).astype(jnp.int32), jax.random.fold_in(streams_of[4], 1), 0, 1),
        "trans": jnp.clip(jax.random.uniform(streams_of[5], (SECTIONS, 2), jnp.float32, -0.3, 0.3) * levels(streams_of[5], (SECTIONS, 2), ((0, 16),), -0.4, 0.0), -0.3, 0.3),
    }


in_stiff = 1.0
anchor_stiff = 0.25
cross_stiff = (0.25, 0.5, 0.5, 0.25)
reaches = (-2, -1, 1, 2)

def spring_force(ext, frac, offsets, fixed, anchor, sec_first, row_first, sections, rows):
    count = fixed.shape[0]
    height = fixed.shape[1]
    width = fixed.shape[2]
    centre = ext[:, 2:count + 2, 3:height + 3, :]
    grow = row_first + jnp.arange(height, dtype=jnp.int32)
    gcol = jnp.arange(width, dtype=jnp.int32)
    gsec = sec_first + jnp.arange(count, dtype=jnp.int32)
    above = ext[:, 2:count + 2, 2:height + 2, :]
    below = ext[:, 2:count + 2, 4:height + 4, :]
    left = jnp.roll(centre, 1, axis=3)
    right = jnp.roll(centre, -1, axis=3)
    force = jnp.where((grow > 0)[:, None], above - centre, 0.0)
    force = force + jnp.where((grow < rows - 1)[:, None], below - centre, 0.0)
    force = force + jnp.where((gcol > 0)[None, :], left - centre, 0.0)
    force = force + jnp.where((gcol < width - 1)[None, :], right - centre, 0.0)
    force = in_stiff * force + anchor_stiff * (jnp.transpose(anchor)[:, :, None, None] - centre)
    for index in range(4):
        reach = reaches[index]
        stiff = cross_stiff[index]
        source = ext[:, 2 + reach:2 + reach + count]

        def pull(block, frow, fcol, shift, own, section):
            frow = frow.astype(jnp.float32)
            fcol = fcol.astype(jnp.float32)
            part_rows = lax.dynamic_slice_in_dim(block, 3 + shift[0], height + 1, 1)
            first = jnp.roll(part_rows, -shift[1], axis=2)
            second = jnp.roll(part_rows, -shift[1] - 1, axis=2)
            match = (1.0 - frow) * ((1.0 - fcol) * first[:, :height] + fcol * second[:, :height])
            match = match + frow * ((1.0 - fcol) * first[:, 1:] + fcol * second[:, 1:])
            flow = jnp.stack([shift[0].astype(jnp.float32) + frow, shift[1].astype(jnp.float32) + fcol])
            gap = match + flow - own
            row_ok = (grow + shift[0] >= 0) & (grow + shift[0] + 1 <= rows - 1)
            col_ok = (gcol + shift[1] >= 0) & (gcol + shift[1] + 1 <= width - 1)
            sec_ok = (section + reach >= 0) & (section + reach < sections)
            valid = row_ok[:, None] & col_ok[None, :] & sec_ok
            return jnp.where(valid, stiff * gap, 0.0)
        force = force + jax.vmap(pull, in_axes=(1, 0, 0, 0, 1, 0), out_axes=1)(source, frac[0, index], frac[1, index], offsets[index], centre, gsec)
    return force * (1 - fixed).astype(jnp.float32)[None]

def reference(displacement, velocity, frac, offsets, fixed, trans):
    anchor = jnp.cumsum(trans, 0)
    keep = (1 - fixed).astype(jnp.float32)
    moving = velocity * keep[None]
    shifted = displacement
    for step in range(ITERS):
        alpha = 0.1 * 0.99 ** step
        delta = 0.25 * 1.1 ** step
        padded = jnp.pad(shifted, ((0, 0), (2, 2), (3, 3), (0, 0)))

        def tile_force(tile_index):
            start = (tile_index * TR).astype(jnp.int32)
            ext = lax.dynamic_slice_in_dim(padded, start, TR + 6, 2)
            piece = lax.dynamic_slice_in_dim(frac, start, TR, 3)
            held = lax.dynamic_slice_in_dim(fixed, start, TR, 1)
            shift = lax.dynamic_index_in_dim(offsets, tile_index, 2, keepdims=False)
            return spring_force(ext, piece, shift, held, anchor, 0, start, SECTIONS, ROWS)
        forces = lax.map(tile_force, jnp.arange(TILES, dtype=jnp.int32))
        force = jnp.moveaxis(forces, 0, 2).reshape(2, SECTIONS, ROWS, COLS)
        ff = jnp.sum(force * force)
        vv = jnp.sum(moving * moving)
        ratio = jnp.sqrt(vv / (ff + 1e-06))
        moving = (1.0 - alpha) * moving + alpha * ratio * force
        moving = moving + delta * force
        shifted = shifted + delta * moving
    return (shifted, moving)
```

```python
import jax
import jax.numpy as jnp
from jax import lax
from jax.experimental import pallas as pl
from jax.experimental.pallas import tpu as pltpu
from jax.sharding import Mesh
from jax.sharding import PartitionSpec as P

ITERS = 3
SEC = ("sec_0", "sec_1", "sec_2")
TILE = ("tile_0", "tile_1")
SEC_TILE = SEC + TILE

in_stiff = 1.0
anchor_stiff = 0.25
cross_stiff = (0.25, 0.5, 0.5, 0.25)
reaches = (-2, -1, 1, 2)
ALPHAS = tuple(0.1 * 0.99**k for k in range(ITERS))
DELTAS = tuple(0.25 * 1.1**k for k in range(ITERS))
UP, DOWN = 2, 3
TINY = 1e-06
NB = 6
PAIRS = [(i, j) for i in range(NB) for j in range(i, NB)]
CANCEL = 1000.0

VMEM = pl.BlockSpec(memory_space=pltpu.VMEM)
SMEM = pl.BlockSpec(memory_space=pltpu.SMEM)


def params():
    return pltpu.CompilerParams(vmem_limit_bytes=48 << 20)


def call(body, out_shape, in_specs, name, flops=4_000_000, bytes_accessed=4_000_000, scratch=()):
    multi = isinstance(out_shape, (list, tuple))
    return pl.pallas_call(
        body,
        out_shape=out_shape,
        in_specs=in_specs,
        out_specs=[VMEM] * len(out_shape) if multi else VMEM,
        scratch_shapes=list(scratch),
        compiler_params=params(),
        cost_estimate=pl.CostEstimate(flops=flops, bytes_accessed=bytes_accessed, transcendentals=0),
        name=name,
    )


def f32(*shape):
    return jax.ShapeDtypeStruct(shape, jnp.float32)


def relayout(u_ref, vel_ref, fixed_ref, out_ref):
    comps, count, height, width = u_ref.shape
    q = width // 128
    for s in range(count):
        for j in range(q):
            cols = pl.ds(128 * j, 128)
            keep = (1 - fixed_ref[s, :, cols]).astype(jnp.float32)
            for c in range(comps):
                rows = pl.ds(j, height, stride=q)
                out_ref.at[0, c, s][rows, :] = u_ref[c, s, :, cols]
                out_ref.at[1, c, s][rows, :] = vel_ref[c, s, :, cols] * keep


def weights(
    place_ref, offsets_ref, anchor_ref, frac_ref, fixed_ref,
    w_ref, diag_ref, keep_ref, base_ref,
):
    count, height, width = fixed_ref.shape
    q = width // 128
    sec_first, row_first, sections, rows = (place_ref[k] for k in range(4))
    grow = row_first + lax.broadcasted_iota(jnp.int32, (height, 128), 0)
    lane = lax.broadcasted_iota(jnp.int32, (height, 128), 1)
    row_links = (grow > 0).astype(jnp.float32) + (grow < rows - 1).astype(jnp.float32)
    for s in range(count):
        shift, row_stiff = [], []
        for i in range(4):
            dr, dc = offsets_ref[i * count * 2 + s * 2], offsets_ref[i * count * 2 + s * 2 + 1]
            other = sec_first + s + reaches[i]
            there = ((other >= 0) & (other < sections)).astype(jnp.float32) * cross_stiff[i]
            row_ok = (grow + dr >= 0) & (grow + dr + 1 <= rows - 1)
            shift.append((dr, dc))
            row_stiff.append(jnp.where(row_ok, there, 0.0))
        for j in range(q):
            cols = pl.ds(128 * j, 128)
            gcol = lane + 128 * j
            keep = (1 - fixed_ref[s, :, cols]).astype(jnp.float32)
            total = jnp.zeros((height, 128), jnp.float32)
            base = [keep * (anchor_stiff * anchor_ref[s * 2 + c]) for c in range(2)]
            at = pl.ds(j, height, stride=q)
            for i in range(4):
                dr, dc = shift[i]
                col_ok = (gcol + dc >= 0) & (gcol + dc + 1 <= width - 1)
                stiff = jnp.where(col_ok, row_stiff[i], 0.0) * keep
                frow = frac_ref[0, i, s, :, cols].astype(jnp.float32)
                fcol = frac_ref[1, i, s, :, cols].astype(jnp.float32)
                low = stiff * frow
                high = stiff - low
                w11 = low * fcol
                w01 = high * fcol
                w_ref.at[s, i, 0][at, :] = high - w01
                w_ref.at[s, i, 1][at, :] = w01
                w_ref.at[s, i, 2][at, :] = low - w11
                w_ref.at[s, i, 3][at, :] = w11
                total = total + stiff
                base[0] = base[0] + stiff * (dr.astype(jnp.float32) + frow)
                base[1] = base[1] + stiff * (dc.astype(jnp.float32) + fcol)
            links = row_links + (gcol > 0).astype(jnp.float32) + (gcol < width - 1).astype(jnp.float32)
            diag_ref.at[s][at, :] = total + keep * (in_stiff * links + anchor_stiff)
            keep_ref.at[s][at, :] = keep * in_stiff
            for c in range(2):
                base_ref.at[c, s][at, :] = base[c]


def apply_springs(offsets_ref, ext, left, right, w, diag, keep, base, out, affine):
    vecs, comps, count, tall, q, lanes = ext.shape
    height = tall - UP - DOWN
    lane = lax.broadcasted_iota(jnp.int32, (q, lanes), 1)
    sub = lax.broadcasted_iota(jnp.int32, (q, lanes), 0)
    first = (sub == 0) & (lane == 0)
    last = (sub == q - 1) & (lane == lanes - 1)
    for s in range(count):
        for r in range(height):
            at = pl.ds(r * q, q)
            kept, own = keep[s, at, :], diag[s, at, :]
            for v in range(vecs):
                for c in range(comps):
                    x = ext[v, c, s, r + UP]
                    before = jnp.where(lane < lanes - 1, x, pltpu.roll(x, 1, 0))
                    after = jnp.where(lane >= 1, x, pltpu.roll(x, q - 1, 0))
                    before = jnp.where(first, 0.0, pltpu.roll(before, 1, 1))
                    after = jnp.where(last, 0.0, pltpu.roll(after, lanes - 1, 1))
                    near = ext[v, c, s, r + UP - 1] + ext[v, c, s, r + UP + 1] + before + after
                    y = kept * near - own * x
                    if affine[v]:
                        y = y + base[c, s, at, :]
                    out[v, c, s, r] = y
        for i in range(4):
            slot = s + 2 + reaches[i]
            source = (left, ext, right)[slot // count]
            index = slot % count
            dr, dc = offsets_ref[i * count * 2 + s * 2], offsets_ref[i * count * 2 + s * 2 + 1]
            ahead = dc >= 0
            turn = jnp.where(ahead, q - 1, 1)
            shift0 = lax.rem(lanes - dc, lanes)
            shift1 = lax.rem(lanes - dc - 1, lanes)
            low0 = jnp.where(ahead, dc, 0)
            high0 = jnp.where(ahead, lanes, lanes + dc)
            low1 = jnp.where(ahead, dc + 1, 0)
            high1 = jnp.where(ahead, lanes, lanes + dc + 1)
            own0 = (lane >= low0) & (lane < high0)
            own1 = (lane >= low1) & (lane < high1)
            held = {}
            for k in range(height + 1):
                if k > 0:
                    at = pl.ds((k - 1) * q, q)
                    w00, w01, w10, w11 = (w[s, i, n, at, :] for n in range(4))
                for v in range(vecs):
                    for c in range(comps):
                        x = source[v, c, index, k + UP + dr]
                        y = pltpu.roll(x, turn, 0)
                        a0 = pltpu.roll(jnp.where(own0, x, y), shift0, 1)
                        a1 = pltpu.roll(jnp.where(own1, x, y), shift1, 1)
                        if k > 0:
                            p0, p1 = held[v, c]
                            term = (w00 * p0 + w01 * p1) + (w10 * a0 + w11 * a1)
                            out[v, c, s, k - 1] += term
                        held[v, c] = (a0, a1)


def springs_body(affine, *refs):
    apply_springs(*refs, affine)


def last_body(devices, offsets, ext, left, right, w, diag, keep, base, start, force, second, out, part):
    apply_springs(offsets, ext, left, right, w, diag, keep, base, out, (False,))
    _, comps, count, height, q, lanes = out.shape
    sums = [jnp.zeros((8, lanes), jnp.float32) for _ in PAIRS]
    for c in range(comps):
        for s in range(count):
            for r in range(height):
                for h in range(q // 8):
                    at = pl.ds(8 * h, 8)
                    vec = (
                        start[1, c, s, r, at, :], force[0, c, s, r, at, :], force[1, c, s, r, at, :],
                        second[0, c, s, r, at, :], second[1, c, s, r, at, :], out[0, c, s, r, at, :],
                    )
                    sums = [g + vec[i] * vec[j] for g, (i, j) in zip(sums, PAIRS)]
    lane = lax.broadcasted_iota(jnp.int32, (1, lanes), 1)
    packed = jnp.zeros((1, lanes), jnp.float32)
    for n, g in enumerate(sums):
        packed = jnp.where(lane == n, jnp.sum(g), packed)
    part[...] = jnp.broadcast_to(packed[None], part.shape)


def coefficients(gram, norms=None):
    zero = jnp.zeros_like(gram[0, 0])
    one = zero + 1.0
    vel = [one] + [zero] * (NB - 1)
    move = [zero] * NB
    force = [zero, one] + [zero] * (NB - 2)
    bad = zero

    def form(x):
        total, size = zero, zero
        for i, j in PAIRS:
            term = x[i] * x[j] * gram[i, j] * (1.0 if i == j else 2.0)
            total, size = total + term, size + jnp.abs(term)
        return jnp.maximum(total, 0.0), size

    for step in range(ITERS):
        alpha, delta = ALPHAS[step], DELTAS[step]
        if norms is None:
            (ff, fs), (vv, vs) = form(force), form(vel)
            lost = (fs > CANCEL * (ff + TINY)) | (vs > CANCEL * (vv + TINY))
            bad = jnp.where(lost, 1.0, bad)
        else:
            ff, vv = norms(force), norms(vel)
        ratio = jnp.sqrt(vv / (ff + TINY))
        gain = alpha * ratio + delta
        vel = [(1.0 - alpha) * a + gain * f for a, f in zip(vel, force)]
        move = [m + delta * a for m, a in zip(move, vel)]
        force = [zero, one] + move[: NB - 2]
    return vel, move, bad


def solve_body(parts, out):
    lanes = parts.shape[-1]
    total = jnp.sum(parts[...], axis=0)
    lane = lax.broadcasted_iota(jnp.int32, (1, lanes), 1)
    gram = {
        pair: jnp.sum(jnp.where(lane == n, total, 0.0), axis=1, keepdims=True)
        for n, pair in enumerate(PAIRS)
    }
    vel, move, bad = coefficients(gram)
    packed = jnp.zeros((1, lanes), jnp.float32)
    for n, value in enumerate(vel + move + [bad]):
        packed = jnp.where(lane == n, value, packed)
    out[...] = packed


def final_body(coef, start, force, second, third, u_ref, v_ref):
    comps, count, height, width = u_ref.shape
    q = width // 128
    vel = [coef[n] for n in range(NB)]
    move = [coef[NB + n] for n in range(NB)]
    for c in range(comps):
        for s in range(count):
            for j in range(q):
                at = pl.ds(j, height, stride=q)
                cols = pl.ds(128 * j, 128)
                vec = (
                    start.at[1, c, s][at, :], force.at[0, c, s][at, :], force.at[1, c, s][at, :],
                    second.at[0, c, s][at, :], second.at[1, c, s][at, :], third.at[0, c, s][at, :],
                )
                u = start.at[0, c, s][at, :]
                v = vel[0] * vec[0]
                u = u + move[0] * vec[0]
                for n in range(1, NB):
                    v = v + vel[n] * vec[n]
                    u = u + move[n] * vec[n]
                u_ref[c, s, :, cols] = u
                v_ref[c, s, :, cols] = v


def neighbours(low_edge, high_edge, axis):
    count = lax.axis_size(axis)
    pairs = [(i, i + 1) for i in range(count - 1)]
    before = lax.ppermute(high_edge, axis, pairs)
    after = lax.ppermute(low_edge, axis, [(b, a) for a, b in pairs])
    return before, after


def exchange(x):
    height = x.shape[3]
    above, below = neighbours(x[:, :, :, :DOWN], x[:, :, :, height - UP :], TILE)
    ext = jnp.concatenate([above, x, below], axis=3)
    left, right = neighbours(ext, ext, SEC)
    return ext, left, right


def sent_to_all(shard, axis):
    count = lax.axis_size(axis)
    return lax.all_to_all(
        jnp.broadcast_to(shard[None], (count, *shard.shape)), axis, 0, 0, tiled=True
    )


def shards(displacement, velocity, frac, offsets, fixed, trans):
    comps, count, height, width = displacement.shape
    q = width // 128
    devices = lax.axis_size(SEC_TILE)
    place = jnp.stack(
        [
            lax.axis_index(SEC) * count,
            lax.axis_index(TILE) * height,
            jnp.int32(count * lax.axis_size(SEC)),
            jnp.int32(height * lax.axis_size(TILE)),
        ]
    ).astype(jnp.int32)
    shifts = offsets.reshape(-1)

    start = call(
        relayout, f32(2, comps, count, height * q, 128), [VMEM] * 3, "relayout"
    )(displacement, velocity, fixed)
    by_row = start.reshape(2, comps, count, height, q, 128)

    local = jnp.cumsum(trans, 0)
    pieces = sent_to_all(local[-1], SEC).reshape(-1, 2)
    passed = jnp.arange(pieces.shape[0]) < lax.axis_index(SEC)
    anchor = local + jnp.sum(jnp.where(passed[:, None], pieces, 0.0), 0)[None]

    w, diag, keep, base = call(
        weights,
        [
            f32(count, 4, 4, height * q, 128),
            f32(count, height * q, 128),
            f32(count, height * q, 128),
            f32(comps, count, height * q, 128),
        ],
        [SMEM] * 3 + [VMEM] * 2,
        "weights",
    )(place, shifts, anchor.reshape(-1), frac, fixed)

    def springs(x, affine, name):
        return call(
            lambda *refs: springs_body(affine, *refs),
            f32(*x.shape),
            [SMEM] + [VMEM] * 7,
            name,
        )(shifts, *exchange(x), w, diag, keep, base)

    force = springs(by_row, (True, False), "force")
    second = springs(force, (False, False), "second")
    third, part = call(
        lambda *refs: last_body(devices, *refs),
        [f32(1, *by_row.shape[1:]), f32(devices, 1, 128)],
        [SMEM] + [VMEM] * 10,
        "third",
    )(shifts, *exchange(second[:1]), w, diag, keep, base, by_row, force, second)

    parts = lax.all_to_all(part, SEC_TILE, 0, 0, tiled=True)
    coef = call(solve_body, f32(1, 128), [VMEM], "solve")(parts)[0]

    def measured(coef):
        basis = (by_row[1], force[0], force[1], second[0], second[1], third[0])

        def norms(x):
            vec = sum(a * b for a, b in zip(x, basis))
            return lax.psum(jnp.sum(vec * vec), SEC_TILE)

        vel, move, _ = coefficients({(0, 0): coef[0] * 0.0}, norms)
        return jnp.concatenate([jnp.stack(vel + move), coef[2 * NB :]])

    coef = lax.cond(coef[2 * NB] > 0.5, measured, lambda coef: coef, coef)

    flat = lambda x: x.reshape(*x.shape[:3], height * q, 128)
    return call(
        final_body,
        [f32(*displacement.shape)] * 2,
        [SMEM] + [VMEM] * 4,
        "final",
    )(coef, start, flat(force), flat(second), flat(third))


def solution(mesh):
    torus = Mesh(
        mesh.devices.reshape(2, 4, 2, 2, 8), ("sec_0", "sec_1", "sec_2", "tile_0", "tile_1")
    )
    in_specs = (
        P(None, SEC, TILE, None),
        P(None, SEC, TILE, None),
        P(None, None, SEC, TILE, None),
        P(None, SEC, TILE, None),
        P(SEC, TILE, None),
        P(SEC, None),
    )
    out_specs = (P(None, SEC, TILE, None), P(None, SEC, TILE, None))
    return jax.shard_map(
        shards, mesh=torus, in_specs=in_specs, out_specs=out_specs, check_vma=False
    )
```

```python
import jax
import jax.numpy as jnp
from jax import lax
from jax.experimental import pallas as pl
from jax.experimental.pallas import tpu as pltpu
from jax.sharding import Mesh
from jax.sharding import PartitionSpec as P


ITERS = 3
SEC = ("sec_0", "sec_1", "sec_2")
TILE = ("tile_0", "tile_1")
SEC_TILE = SEC + TILE

in_stiff = 1.0
anchor_stiff = 0.25
cross_stiff = (0.25, 0.5, 0.5, 0.25)
reaches = (-2, -1, 1, 2)
ALPHAS = tuple(0.1 * 0.99**k for k in range(ITERS))
DELTAS = tuple(0.25 * 1.1**k for k in range(ITERS))
UP, DOWN = 2, 3
TINY = 1e-06
NB = 6
PAIRS = [(i, j) for i in range(NB) for j in range(i, NB)]
CANCEL = 1000.0

VMEM = pl.BlockSpec(memory_space=pltpu.VMEM)
SMEM = pl.BlockSpec(memory_space=pltpu.SMEM)
HBM = pl.BlockSpec(memory_space=pltpu.HBM)


def params():
    return pltpu.CompilerParams(vmem_limit_bytes=48 << 20)


def call(body, out_shape, in_specs, flops=4_000_000, bytes_accessed=4_000_000, scratch=()):
    multi = isinstance(out_shape, (list, tuple))
    return pl.pallas_call(
        body,
        out_shape=out_shape,
        in_specs=in_specs,
        out_specs=[VMEM] * len(out_shape) if multi else VMEM,
        scratch_shapes=list(scratch),
        compiler_params=params(),
        cost_estimate=pl.CostEstimate(flops=flops, bytes_accessed=bytes_accessed, transcendentals=0),
    )


def f32(*shape):
    return jax.ShapeDtypeStruct(shape, jnp.float32)


def relayout(u_hbm, vel_hbm, fixed_hbm, out_ref, u_ref, vel_ref, fixed_ref, sems):
    copies = [
        pltpu.make_async_copy(a, b, sems.at[n])
        for n, (a, b) in enumerate(
            ((u_hbm, u_ref), (vel_hbm, vel_ref), (fixed_hbm, fixed_ref))
        )
    ]
    for copy in copies:
        copy.start()
    for copy in copies:
        copy.wait()
    comps, count, height, width = u_ref.shape
    q = width // 128
    for s in range(count):
        for j in range(q):
            cols = pl.ds(128 * j, 128)
            keep = (1 - fixed_ref[s, :, cols]).astype(jnp.float32)
            for c in range(comps):
                rows = pl.ds(j, height, stride=q)
                out_ref.at[0, c, s][rows, :] = u_ref[c, s, :, cols]
                out_ref.at[1, c, s][rows, :] = vel_ref[c, s, :, cols] * keep


def weights(
    place_ref, offsets_ref, anchor_ref, frac_ref, fixed_ref,
    w_ref, diag_ref, keep_ref, base_ref,
):
    count, height, width = fixed_ref.shape
    q = width // 128
    sec_first, row_first, sections, rows = (place_ref[k] for k in range(4))
    grow = row_first + lax.broadcasted_iota(jnp.int32, (height, 128), 0)
    lane = lax.broadcasted_iota(jnp.int32, (height, 128), 1)
    row_links = (grow > 0).astype(jnp.float32) + (grow < rows - 1).astype(jnp.float32)
    for s in range(count):
        shift, row_stiff = [], []
        for i in range(4):
            dr, dc = offsets_ref[i * count * 2 + s * 2], offsets_ref[i * count * 2 + s * 2 + 1]
            other = sec_first + s + reaches[i]
            there = ((other >= 0) & (other < sections)).astype(jnp.float32) * cross_stiff[i]
            row_ok = (grow + dr >= 0) & (grow + dr + 1 <= rows - 1)
            shift.append((dr, dc))
            row_stiff.append(jnp.where(row_ok, there, 0.0))
        for j in range(q):
            cols = pl.ds(128 * j, 128)
            gcol = lane + 128 * j
            keep = (1 - fixed_ref[s, :, cols]).astype(jnp.float32)
            total = jnp.zeros((height, 128), jnp.float32)
            base = [keep * (anchor_stiff * anchor_ref[s * 2 + c]) for c in range(2)]
            at = pl.ds(j, height, stride=q)
            for i in range(4):
                dr, dc = shift[i]
                col_ok = (gcol + dc >= 0) & (gcol + dc + 1 <= width - 1)
                stiff = jnp.where(col_ok, row_stiff[i], 0.0) * keep
                frow = frac_ref[0, i, s, :, cols].astype(jnp.float32)
                fcol = frac_ref[1, i, s, :, cols].astype(jnp.float32)
                low = stiff * frow
                high = stiff - low
                w11 = low * fcol
                w01 = high * fcol
                w_ref.at[s, i, 0][at, :] = high - w01
                w_ref.at[s, i, 1][at, :] = w01
                w_ref.at[s, i, 2][at, :] = low - w11
                w_ref.at[s, i, 3][at, :] = w11
                total = total + stiff
                base[0] = base[0] + stiff * (dr.astype(jnp.float32) + frow)
                base[1] = base[1] + stiff * (dc.astype(jnp.float32) + fcol)
            links = row_links + (gcol > 0).astype(jnp.float32) + (gcol < width - 1).astype(jnp.float32)
            diag_ref.at[s][at, :] = total + keep * (in_stiff * links + anchor_stiff)
            keep_ref.at[s][at, :] = keep * in_stiff
            for c in range(2):
                base_ref.at[c, s][at, :] = base[c]


def stay(ext, diag, keep, base, out, affine):
    vecs, comps, count, tall, q, lanes = ext.shape
    height = tall - UP - DOWN
    lane = lax.broadcasted_iota(jnp.int32, (q, lanes), 1)
    sub = lax.broadcasted_iota(jnp.int32, (q, lanes), 0)
    first = (sub == 0) & (lane == 0)
    last = (sub == q - 1) & (lane == lanes - 1)
    for s in range(count):
        for r in range(height):
            at = pl.ds(r * q, q)
            kept, own = keep[s, at, :], diag[s, at, :]
            for v in range(vecs):
                for c in range(comps):
                    x = ext[v, c, s, r + UP]
                    before = jnp.where(lane < lanes - 1, x, pltpu.roll(x, 1, 0))
                    after = jnp.where(lane >= 1, x, pltpu.roll(x, q - 1, 0))
                    before = jnp.where(first, 0.0, pltpu.roll(before, 1, 1))
                    after = jnp.where(last, 0.0, pltpu.roll(after, lanes - 1, 1))
                    near = ext[v, c, s, r + UP - 1] + ext[v, c, s, r + UP + 1] + before + after
                    y = kept * near - own * x
                    if affine[v]:
                        y = y + base[c, s, at, :]
                    out[v, c, s, r] = y


def pull(offsets_ref, source, index, s, i, w, out):
    vecs, comps, count, tall, q, lanes = source.shape
    height = tall - UP - DOWN
    lane = lax.broadcasted_iota(jnp.int32, (q, lanes), 1)
    spot = i * (count * 2) + s * 2
    dr, dc = offsets_ref[spot], offsets_ref[spot + 1]
    ahead = dc >= 0
    turn = jnp.where(ahead, q - 1, 1)
    shift0 = lax.rem(lanes - dc, lanes)
    shift1 = lax.rem(lanes - dc - 1, lanes)
    low0 = jnp.where(ahead, dc, 0)
    high0 = jnp.where(ahead, lanes, lanes + dc)
    low1 = jnp.where(ahead, dc + 1, 0)
    high1 = jnp.where(ahead, lanes, lanes + dc + 1)
    own0 = (lane >= low0) & (lane < high0)
    own1 = (lane >= low1) & (lane < high1)
    held = {}
    for k in range(height + 1):
        if k > 0:
            at = pl.ds((k - 1) * q, q)
            w00, w01, w10, w11 = (w[s, i, n, at, :] for n in range(4))
        for v in range(vecs):
            for c in range(comps):
                x = source[v, c, index, k + UP + dr]
                y = pltpu.roll(x, turn, 0)
                a0 = pltpu.roll(jnp.where(own0, x, y), shift0, 1)
                a1 = pltpu.roll(jnp.where(own1, x, y), shift1, 1)
                if k > 0:
                    p0, p1 = held[v, c]
                    term = (w00 * p0 + w01 * p1) + (w10 * a0 + w11 * a1)
                    out[v, c, s, k - 1] += term
                held[v, c] = (a0, a1)


def pull_pair(odd, offsets, source, w, out):
    for behind, ahead in (((0, 0, 0), (0, 3, 0)), ((0, 1, 1), (1, 2, 0)), ((1, 0, 1), (1, 3, 1))):
        s, i, index = (jnp.where(odd, b, a) for a, b in zip(behind, ahead))
        pull(offsets, source, index, s, i, w, out)


def near_body(affine, place, offsets, ext, chip, w, diag, keep, base, out):
    stay(ext, diag, keep, base, out, affine)
    pull(offsets, ext, 1, 0, 2, w, out)
    pull(offsets, ext, 0, 1, 1, w, out)
    pull_pair(place[4] == 0, offsets, chip, w, out)


def far_body(place, offsets, part, link, w, out):
    out[...] = part[...]
    pull_pair(place[4] == 1, offsets, link, w, out)


def products(pairs, blocks):
    comps, count, height, q, lanes = next(iter(blocks.values()))[0].shape[1:]
    sums = [jnp.zeros((8, lanes), jnp.float32) for _ in pairs]
    for c in range(comps):
        for s in range(count):
            for r in range(height):
                for h in range(q // 8):
                    at = pl.ds(8 * h, 8)
                    vec = {n: ref[v, c, s, r, at, :] for n, (ref, v) in blocks.items()}
                    sums = [g + vec[i] * vec[j] for g, (i, j) in zip(sums, pairs)]
    lane = lax.broadcasted_iota(jnp.int32, (1, lanes), 1)
    packed = jnp.zeros((1, lanes), jnp.float32)
    for pair, g in zip(pairs, sums):
        packed = jnp.where(lane == PAIRS.index(pair), jnp.sum(g), packed)
    return packed


EARLY = [pair for pair in PAIRS if pair[1] < NB - 1]
LATE = [pair for pair in PAIRS if pair[1] == NB - 1]


def basis(start, force, second):
    return {0: (start, 1), 1: (force, 0), 2: (force, 1), 3: (second, 0), 4: (second, 1)}


def near_last_body(place, offsets, ext, chip, w, diag, keep, base, start, force, second, out, early):
    near_body((False,), place, offsets, ext, chip, w, diag, keep, base, out)
    early[...] = products(EARLY, basis(start, force, second))


def far_last_body(place, offsets, part, link, w, early, start, force, second, out, sums):
    far_body(place, offsets, part, link, w, out)
    late = products(LATE, {**basis(start, force, second), NB - 1: (out, 0)})
    sums[...] = jnp.broadcast_to((early[...] + late)[None], sums.shape)


def coefficients(gram, norms=None):
    zero = jnp.zeros_like(gram[0, 0])
    one = zero + 1.0
    vel = [one] + [zero] * (NB - 1)
    move = [zero] * NB
    force = [zero, one] + [zero] * (NB - 2)
    bad = zero

    def form(x):
        total, size = zero, zero
        for i, j in PAIRS:
            term = x[i] * x[j] * gram[i, j] * (1.0 if i == j else 2.0)
            total, size = total + term, size + jnp.abs(term)
        return jnp.maximum(total, 0.0), size

    for step in range(ITERS):
        alpha, delta = ALPHAS[step], DELTAS[step]
        if norms is None:
            (ff, fs), (vv, vs) = form(force), form(vel)
            lost = (fs > CANCEL * (ff + TINY)) | (vs > CANCEL * (vv + TINY))
            bad = jnp.where(lost, 1.0, bad)
        else:
            ff, vv = norms(force), norms(vel)
        ratio = jnp.sqrt(vv / (ff + TINY))
        gain = alpha * ratio + delta
        vel = [(1.0 - alpha) * a + gain * f for a, f in zip(vel, force)]
        move = [m + delta * a for m, a in zip(move, vel)]
        force = [zero, one] + move[: NB - 2]
    return vel, move, bad


def solve_body(parts, out):
    lanes = parts.shape[-1]
    total = jnp.sum(parts[...], axis=0)
    lane = lax.broadcasted_iota(jnp.int32, (1, lanes), 1)
    gram = {
        pair: jnp.sum(jnp.where(lane == n, total, 0.0), axis=1, keepdims=True)
        for n, pair in enumerate(PAIRS)
    }
    vel, move, bad = coefficients(gram)
    packed = jnp.zeros((1, lanes), jnp.float32)
    for n, value in enumerate(vel + move + [bad]):
        packed = jnp.where(lane == n, value, packed)
    out[...] = packed


def final_body(coef, start, force, second, third, u_ref, v_ref):
    comps, count, height, width = u_ref.shape
    q = width // 128
    vel = [coef[n] for n in range(NB)]
    move = [coef[NB + n] for n in range(NB)]
    for c in range(comps):
        for s in range(count):
            for j in range(q):
                at = pl.ds(j, height, stride=q)
                cols = pl.ds(128 * j, 128)
                vec = (
                    start.at[1, c, s][at, :], force.at[0, c, s][at, :], force.at[1, c, s][at, :],
                    second.at[0, c, s][at, :], second.at[1, c, s][at, :], third.at[0, c, s][at, :],
                )
                u = start.at[0, c, s][at, :]
                v = vel[0] * vec[0]
                u = u + move[0] * vec[0]
                for n in range(1, NB):
                    v = v + vel[n] * vec[n]
                    u = u + move[n] * vec[n]
                u_ref[c, s, :, cols] = u
                v_ref[c, s, :, cols] = v


def swapped(x, axis, first):
    pairs = []
    for i in range(first, lax.axis_size(axis) - 1, 2):
        pairs += [(i, i + 1), (i + 1, i)]
    return lax.ppermute(x, axis, pairs)


def taller(x):
    height = x.shape[3]
    odd = lax.axis_index(TILE) % 2 == 1
    top = lambda a: lax.dynamic_slice_in_dim(x, jnp.where(a, 0, height - DOWN), DOWN, 3)
    outer = swapped(top(~odd), TILE, 1)
    inner = swapped(top(odd), TILE, 0)
    above = jnp.where(odd, inner, outer)[:, :, :, DOWN - UP :]
    below = jnp.where(odd, outer, inner)
    return jnp.concatenate([above, x, below], axis=3)


def across(ext):
    link = swapped(ext, SEC, 1)
    chip = swapped(ext, SEC, 0)
    return chip, link


def sent_to_all(shard, axis):
    count = lax.axis_size(axis)
    return lax.all_to_all(
        jnp.broadcast_to(shard[None], (count, *shard.shape)), axis, 0, 0, tiled=True
    )


def shards(displacement, velocity, frac, offsets, fixed, trans):
    comps, count, height, width = displacement.shape
    q = width // 128
    devices = lax.axis_size(SEC_TILE)
    place = jnp.stack(
        [
            lax.axis_index(SEC) * count,
            lax.axis_index(TILE) * height,
            jnp.int32(count * lax.axis_size(SEC)),
            jnp.int32(height * lax.axis_size(TILE)),
            lax.axis_index(SEC) % 2,
        ]
    ).astype(jnp.int32)
    shifts = offsets.reshape(-1)

    start = call(
        relayout,
        f32(2, comps, count, height * q, 128),
        [HBM] * 3,
        scratch=[
            pltpu.VMEM(displacement.shape, jnp.float32),
            pltpu.VMEM(displacement.shape, jnp.float32),
            pltpu.VMEM(fixed.shape, jnp.int32),
            pltpu.SemaphoreType.DMA((3,)),
        ],
    )(displacement, velocity, fixed)
    by_row = start.reshape(2, comps, count, height, q, 128)

    local = jnp.cumsum(trans, 0)
    pieces = sent_to_all(local[-1], SEC).reshape(-1, 2)
    passed = jnp.arange(pieces.shape[0]) < lax.axis_index(SEC)
    anchor = local + jnp.sum(jnp.where(passed[:, None], pieces, 0.0), 0)[None]

    w, diag, keep, base = call(
        weights,
        [
            f32(count, 4, 4, height * q, 128),
            f32(count, height * q, 128),
            f32(count, height * q, 128),
            f32(comps, count, height * q, 128),
        ],
        [SMEM] * 3 + [VMEM] * 2,
    )(place, shifts, anchor.reshape(-1), frac, fixed)

    def springs(x, affine):
        ext = taller(x)
        chip, link = across(ext)
        part = call(
            lambda *refs: near_body(affine, *refs), f32(*x.shape), [SMEM] * 2 + [VMEM] * 6
        )(place, shifts, ext, chip, w, diag, keep, base)
        return call(far_body, f32(*x.shape), [SMEM] * 2 + [VMEM] * 3)(place, shifts, part, link, w)

    force = springs(by_row, (True, False))
    second = springs(force, (False, False))
    ext = taller(second[:1])
    chip, link = across(ext)
    third, early = call(
        near_last_body, [f32(*second[:1].shape), f32(1, 128)], [SMEM] * 2 + [VMEM] * 9
    )(place, shifts, ext, chip, w, diag, keep, base, by_row, force, second)
    third, part = call(
        far_last_body, [f32(*third.shape), f32(devices, 1, 128)], [SMEM] * 2 + [VMEM] * 7
    )(place, shifts, third, link, w, early, by_row, force, second)

    parts = lax.all_to_all(part, SEC_TILE, 0, 0, tiled=True)
    coef = call(solve_body, f32(1, 128), [VMEM])(parts)[0]

    def measured(coef):
        basis = (by_row[1], force[0], force[1], second[0], second[1], third[0])

        def norms(x):
            vec = sum(a * b for a, b in zip(x, basis))
            return lax.psum(jnp.sum(vec * vec), SEC_TILE)

        vel, move, _ = coefficients({(0, 0): coef[0] * 0.0}, norms)
        return jnp.concatenate([jnp.stack(vel + move), coef[2 * NB :]])

    coef = lax.cond(coef[2 * NB] > 0.5, measured, lambda coef: coef, coef)

    flat = lambda x: x.reshape(*x.shape[:3], height * q, 128)
    return call(
        final_body, [f32(*displacement.shape)] * 2, [SMEM] + [VMEM] * 4
    )(coef, start, flat(force), flat(second), flat(third))


def solution(mesh):
    torus = Mesh(
        mesh.devices.reshape(2, 4, 2, 2, 8), ("sec_0", "sec_1", "sec_2", "tile_0", "tile_1")
    )
    in_specs = (
        P(None, SEC, TILE, None),
        P(None, SEC, TILE, None),
        P(None, None, SEC, TILE, None),
        P(None, SEC, TILE, None),
        P(SEC, TILE, None),
        P(SEC, None),
    )
    out_specs = (P(None, SEC, TILE, None), P(None, SEC, TILE, None))
    return jax.shard_map(
        shards, mesh=torus, in_specs=in_specs, out_specs=out_specs, check_vma=False
    )
```

```python
import jax
import jax.numpy as jnp
from jax import lax
from jax.experimental import pallas as pl
from jax.experimental.pallas import tpu as pltpu
from jax.sharding import Mesh
from jax.sharding import PartitionSpec as P


ITERS = 3
SEC = ("sec_0", "sec_1", "sec_2")
TILE = ("tile_0", "tile_1")
SEC_TILE = SEC + TILE

in_stiff = 1.0
anchor_stiff = 0.25
cross_stiff = (0.25, 0.5, 0.5, 0.25)
reaches = (-2, -1, 1, 2)
ALPHAS = tuple(0.1 * 0.99**k for k in range(ITERS))
DELTAS = tuple(0.25 * 1.1**k for k in range(ITERS))
UP, DOWN = 2, 3
TINY = 1e-06
NB = 6
PAIRS = [(i, j) for i in range(NB) for j in range(i, NB)]
CANCEL = 1000.0

VMEM = pl.BlockSpec(memory_space=pltpu.VMEM)
SMEM = pl.BlockSpec(memory_space=pltpu.SMEM)
HBM = pl.BlockSpec(memory_space=pltpu.HBM)
FULL = (64 << 20) - (1280 << 10)


def call(body, out_shape, in_specs, flops=4_000_000, bytes_accessed=4_000_000, scratch=(), vmem=16 << 20):
    multi = isinstance(out_shape, (list, tuple))
    return pl.pallas_call(
        body,
        out_shape=out_shape,
        in_specs=in_specs,
        out_specs=[VMEM] * len(out_shape) if multi else VMEM,
        scratch_shapes=list(scratch),
        compiler_params=pltpu.CompilerParams(vmem_limit_bytes=vmem),
        cost_estimate=pl.CostEstimate(flops=flops, bytes_accessed=bytes_accessed, transcendentals=0),
    )


def f32(*shape):
    return jax.ShapeDtypeStruct(shape, jnp.float32)


def relayout(u_hbm, vel_hbm, fixed_hbm, out_ref, u_ref, vel_ref, fixed_ref, sems):
    copies = [
        pltpu.make_async_copy(a, b, sems.at[n])
        for n, (a, b) in enumerate(
            ((u_hbm, u_ref), (vel_hbm, vel_ref), (fixed_hbm, fixed_ref))
        )
    ]
    for copy in copies:
        copy.start()
    for copy in copies:
        copy.wait()
    comps, count, height, width = u_ref.shape
    q = width // 128
    for s in range(count):
        for j in range(q):
            cols = pl.ds(128 * j, 128)
            keep = (1 - fixed_ref[s, :, cols]).astype(jnp.float32)
            for c in range(comps):
                rows = pl.ds(j, height, stride=q)
                out_ref.at[0, c, s][rows, :] = u_ref[c, s, :, cols]
                out_ref.at[1, c, s][rows, :] = vel_ref[c, s, :, cols] * keep


def weights(
    place_ref, offsets_ref, frac_ref, fixed_ref,
    w_ref, diag_ref, keep_ref, base_ref, frac,
):
    count, height, width = fixed_ref.shape
    q = width // 128
    sec_first, row_first, sections, rows = (place_ref[k] for k in range(4))
    for s in range(count):
        for j in range(q):
            cols = pl.ds(128 * j, 128)
            at = pl.ds(j, height, stride=q)
            keep_ref.at[s][at, :] = (1 - fixed_ref[s, :, cols]).astype(jnp.float32)
            for i in range(4):
                for c in range(2):
                    frac.at[c, i][at, :] = frac_ref[c, i, s, :, cols].astype(jnp.float32)
        sub = lax.broadcasted_iota(jnp.int32, (q, 128), 0)
        gcol = lax.broadcasted_iota(jnp.int32, (q, 128), 1) + 128 * sub
        col_links = (gcol > 0).astype(jnp.float32) + (gcol < width - 1).astype(jnp.float32)
        springs = []
        for i in range(4):
            dr, dc = offsets_ref[i * count * 2 + s * 2], offsets_ref[i * count * 2 + s * 2 + 1]
            other = sec_first + s + reaches[i]
            there = (other >= 0) & (other < sections)
            col_ok = (gcol + dc >= 0) & (gcol + dc + 1 <= width - 1) & there
            springs.append((dr, dc, jnp.where(col_ok, cross_stiff[i], 0.0)))
        for r in range(height):
            at = pl.ds(r * q, q)
            grow = row_first + r
            row_links = jnp.where(grow > 0, 1.0, 0.0) + jnp.where(grow < rows - 1, 1.0, 0.0)
            keep = keep_ref[s, at, :]
            total = keep * (in_stiff * (row_links + col_links) + anchor_stiff)
            base = [jnp.zeros((q, 128), jnp.float32) for _ in range(2)]
            for i in range(4):
                dr, dc, col_stiff = springs[i]
                row_ok = (grow + dr >= 0) & (grow + dr + 1 <= rows - 1)
                stiff = col_stiff * keep * jnp.where(row_ok, 1.0, 0.0)
                frow, fcol = frac[0, i, at, :], frac[1, i, at, :]
                low = stiff * frow
                high = stiff - low
                w11 = low * fcol
                w01 = high * fcol
                w_ref[s, i, 0, at, :] = high - w01
                w_ref[s, i, 1, at, :] = w01
                w_ref[s, i, 2, at, :] = low - w11
                w_ref[s, i, 3, at, :] = w11
                total = total + stiff
                base[0] = base[0] + stiff * (dr.astype(jnp.float32) + frow)
                base[1] = base[1] + stiff * (dc.astype(jnp.float32) + fcol)
            diag_ref[s, at, :] = total
            for c in range(2):
                base_ref[c, s, at, :] = base[c]


def stay(ext, diag, keep, base, out, affine):
    vecs, comps, count, tall, q, lanes = ext.shape
    height = tall - UP - DOWN
    lane = lax.broadcasted_iota(jnp.int32, (q, lanes), 1)
    sub = lax.broadcasted_iota(jnp.int32, (q, lanes), 0)
    first = (sub == 0) & (lane == 0)
    last = (sub == q - 1) & (lane == lanes - 1)
    for s in range(count):
        for r in range(height):
            at = pl.ds(r * q, q)
            kept, own = keep[s, at, :], diag[s, at, :]
            for v in range(vecs):
                for c in range(comps):
                    x = ext[v, c, s, r + UP]
                    before = jnp.where(lane < lanes - 1, x, pltpu.roll(x, 1, 0))
                    after = jnp.where(lane >= 1, x, pltpu.roll(x, q - 1, 0))
                    before = jnp.where(first, 0.0, pltpu.roll(before, 1, 1))
                    after = jnp.where(last, 0.0, pltpu.roll(after, lanes - 1, 1))
                    near = in_stiff * (ext[v, c, s, r + UP - 1] + ext[v, c, s, r + UP + 1] + before + after)
                    y = kept * near - own * x
                    if affine[v]:
                        y = y + base[c, s, at, :]
                    out[v, c, s, r] = y


def pull(offsets_ref, source, index, s, i, w, out):
    vecs, comps, count, tall, q, lanes = source.shape
    height = tall - UP - DOWN
    lane = lax.broadcasted_iota(jnp.int32, (q, lanes), 1)
    spot = i * (count * 2) + s * 2
    dr, dc = offsets_ref[spot], offsets_ref[spot + 1]
    ahead = dc >= 0
    turn = jnp.where(ahead, q - 1, 1)
    shift0 = lax.rem(lanes - dc, lanes)
    shift1 = lax.rem(lanes - dc - 1, lanes)
    low0 = jnp.where(ahead, dc, 0)
    high0 = jnp.where(ahead, lanes, lanes + dc)
    low1 = jnp.where(ahead, dc + 1, 0)
    high1 = jnp.where(ahead, lanes, lanes + dc + 1)
    own0 = (lane >= low0) & (lane < high0)
    own1 = (lane >= low1) & (lane < high1)
    held = {}
    for k in range(height + 1):
        if k > 0:
            at = pl.ds((k - 1) * q, q)
            w00, w01, w10, w11 = (w[s, i, n, at, :] for n in range(4))
        for v in range(vecs):
            for c in range(comps):
                x = source[v, c, index, k + UP + dr]
                y = pltpu.roll(x, turn, 0)
                a0 = pltpu.roll(jnp.where(own0, x, y), shift0, 1)
                a1 = pltpu.roll(jnp.where(own1, x, y), shift1, 1)
                if k > 0:
                    p0, p1 = held[v, c]
                    term = (w00 * p0 + w01 * p1) + (w10 * a0 + w11 * a1)
                    out[v, c, s, k - 1] += term
                held[v, c] = (a0, a1)


def pull_pair(odd, offsets, source, w, out):
    for behind, ahead in (((0, 0, 0), (0, 3, 0)), ((0, 1, 1), (1, 2, 0)), ((1, 0, 1), (1, 3, 1))):
        s, i, index = (jnp.where(odd, b, a) for a, b in zip(behind, ahead))
        pull(offsets, source, index, s, i, w, out)


def near_body(affine, place, offsets, ext, chip, w, diag, keep, base, out):
    stay(ext, diag, keep, base, out, affine)
    pull(offsets, ext, 1, 0, 2, w, out)
    pull(offsets, ext, 0, 1, 1, w, out)
    pull_pair(place[4] == 0, offsets, chip, w, out)


def far_body(place, offsets, part, link, w, out):
    out[...] = part[...]
    pull_pair(place[4] == 1, offsets, link, w, out)


def far_first_body(place, offsets, anchor, part, link, w, keep, out):
    _, comps, count, height, q, _ = out.shape
    out[1:] = part[1:]
    for s in range(count):
        for c in range(comps):
            pulled = anchor_stiff * anchor[s, c]
            for r in range(height):
                out[0, c, s, r] = part[0, c, s, r] + keep[s, pl.ds(r * q, q), :] * pulled
    pull_pair(place[4] == 1, offsets, link, w, out)


def products(pairs, blocks):
    comps, count, height, q, lanes = next(iter(blocks.values()))[0].shape[1:]
    sums = [jnp.zeros((8, lanes), jnp.float32) for _ in pairs]
    for c in range(comps):
        for s in range(count):
            for r in range(height):
                for h in range(q // 8):
                    at = pl.ds(8 * h, 8)
                    vec = {n: ref[v, c, s, r, at, :] for n, (ref, v) in blocks.items()}
                    sums = [g + vec[i] * vec[j] for g, (i, j) in zip(sums, pairs)]
    lane = lax.broadcasted_iota(jnp.int32, (1, lanes), 1)
    packed = jnp.zeros((1, lanes), jnp.float32)
    for pair, g in zip(pairs, sums):
        packed = jnp.where(lane == PAIRS.index(pair), jnp.sum(g), packed)
    return packed


EARLY = [pair for pair in PAIRS if pair[1] < NB - 1]
LATE = [pair for pair in PAIRS if pair[1] == NB - 1]


def basis(start, force, second):
    return {0: (start, 1), 1: (force, 0), 2: (force, 1), 3: (second, 0), 4: (second, 1)}


def near_last_body(place, offsets, ext, chip, w, diag, keep, base, start, force, second, out, early):
    near_body((False,), place, offsets, ext, chip, w, diag, keep, base, out)
    early[...] = products(EARLY, basis(start, force, second))


def far_last_body(place, offsets, part, link, w, early, start, force, second, out, sums):
    far_body(place, offsets, part, link, w, out)
    late = products(LATE, {**basis(start, force, second), NB - 1: (out, 0)})
    sums[...] = jnp.broadcast_to((early[...] + late)[None], sums.shape)


def coefficients(gram, norms=None):
    zero = jnp.zeros_like(gram[0, 0])
    one = zero + 1.0
    vel = [one] + [zero] * (NB - 1)
    move = [zero] * NB
    force = [zero, one] + [zero] * (NB - 2)
    bad = zero

    def form(x):
        total, size = zero, zero
        for i, j in PAIRS:
            term = x[i] * x[j] * gram[i, j] * (1.0 if i == j else 2.0)
            total, size = total + term, size + jnp.abs(term)
        return jnp.maximum(total, 0.0), size

    for step in range(ITERS):
        alpha, delta = ALPHAS[step], DELTAS[step]
        if norms is None:
            (ff, fs), (vv, vs) = form(force), form(vel)
            lost = (fs > CANCEL * (ff + TINY)) | (vs > CANCEL * (vv + TINY))
            bad = jnp.where(lost, 1.0, bad)
        else:
            ff, vv = norms(force), norms(vel)
        ratio = jnp.sqrt(vv / (ff + TINY))
        gain = alpha * ratio + delta
        vel = [(1.0 - alpha) * a + gain * f for a, f in zip(vel, force)]
        move = [m + delta * a for m, a in zip(move, vel)]
        force = [zero, one] + move[: NB - 2]
    return vel, move, bad


def solve_body(parts, out):
    lanes = parts.shape[-1]
    total = jnp.sum(parts[...], axis=0)
    lane = lax.broadcasted_iota(jnp.int32, (1, lanes), 1)
    gram = {
        pair: jnp.sum(jnp.where(lane == n, total, 0.0), axis=1, keepdims=True)
        for n, pair in enumerate(PAIRS)
    }
    vel, move, bad = coefficients(gram)
    packed = jnp.zeros((1, lanes), jnp.float32)
    for n, value in enumerate(vel + move + [bad]):
        packed = jnp.where(lane == n, value, packed)
    out[...] = packed


def final_body(coef, start, force, second, third, u_ref, v_ref, flat):
    comps, count, height, width = u_ref.shape
    q = width // 128
    vel = [coef[n] for n in range(NB)]
    move = [coef[NB + n] for n in range(NB)]
    blocks = ((start, 1), (force, 0), (force, 1), (second, 0), (second, 1), (third, 0))
    for c in range(comps):
        for s in range(count):
            for r in range(height):
                at = pl.ds(r * q, q)
                vec = [ref[n, c, s, at, :] for ref, n in blocks]
                u = start[0, c, s, at, :]
                v = vel[0] * vec[0]
                u = u + move[0] * vec[0]
                for n in range(1, NB):
                    v = v + vel[n] * vec[n]
                    u = u + move[n] * vec[n]
                flat[0, at, :] = u
                flat[1, at, :] = v
            for j in range(q):
                at = pl.ds(j, height, stride=q)
                u_ref[c, s, :, pl.ds(128 * j, 128)] = flat.at[0][at, :]
                v_ref[c, s, :, pl.ds(128 * j, 128)] = flat.at[1][at, :]


def swapped(x, axis, first):
    pairs = []
    for i in range(first, lax.axis_size(axis) - 1, 2):
        pairs += [(i, i + 1), (i + 1, i)]
    return lax.ppermute(x, axis, pairs)


def exchange(x, first=()):
    height = x.shape[3]
    odd = lax.axis_index(TILE) % 2 == 1
    edge = lambda top: lax.dynamic_slice_in_dim(x, jnp.where(top, 0, height - DOWN), DOWN, 3)
    outer = swapped(edge(~odd), TILE, 1)
    inner = swapped(edge(odd), TILE, 0)
    link = swapped(lax.optimization_barrier((x, *first))[0] if first else x, SEC, 1)
    above = jnp.where(odd, inner, outer)[:, :, :, DOWN - UP :]
    below = jnp.where(odd, outer, inner)
    edges = jnp.concatenate([above, below], axis=3)
    link_edges = swapped(edges, SEC, 1)
    ext = jnp.concatenate([above, x, below], axis=3)
    chip = swapped(ext, SEC, 0)
    link = jnp.concatenate([link_edges[:, :, :, :UP], link, link_edges[:, :, :, UP:]], axis=3)
    return ext, chip, link


def shards(displacement, velocity, frac, offsets, fixed, trans):
    comps, count, height, width = displacement.shape
    q = width // 128
    devices = lax.axis_size(SEC_TILE)
    place = jnp.stack(
        [
            lax.axis_index(SEC) * count,
            lax.axis_index(TILE) * height,
            jnp.int32(count * lax.axis_size(SEC)),
            jnp.int32(height * lax.axis_size(TILE)),
            lax.axis_index(SEC) % 2,
        ]
    ).astype(jnp.int32)
    shifts = offsets.reshape(-1)

    start = call(
        relayout,
        f32(2, comps, count, height * q, 128),
        [HBM] * 3,
        scratch=[
            pltpu.VMEM(displacement.shape, jnp.float32),
            pltpu.VMEM(displacement.shape, jnp.float32),
            pltpu.VMEM(fixed.shape, jnp.int32),
            pltpu.SemaphoreType.DMA((3,)),
        ],
        vmem=FULL,
    )(displacement, velocity, fixed)
    by_row = start.reshape(2, comps, count, height, q, 128)

    local = jnp.cumsum(trans, 0)
    group = lax.axis_size(SEC)
    pieces = lax.all_to_all(
        jnp.broadcast_to(local[-1][None, None], (group, 1, 2)), SEC, 0, 0, tiled=True
    )
    passed = jnp.arange(group) < lax.axis_index(SEC)
    anchor = local + jnp.sum(jnp.where(passed[:, None], pieces[:, 0], 0.0), 0)[None]

    w, diag, keep, base = call(
        weights,
        [
            f32(count, 4, 4, height * q, 128),
            f32(count, height * q, 128),
            f32(count, height * q, 128),
            f32(comps, count, height * q, 128),
        ],
        [SMEM] * 2 + [VMEM] * 2,
        scratch=[pltpu.VMEM((2, 4, height * q, 128), jnp.float32)],
    )(place, shifts, frac, fixed)

    def near(x, ext, chip, affine):
        return call(
            lambda *refs: near_body(affine, *refs), f32(*x.shape), [SMEM] * 2 + [VMEM] * 6
        )(place, shifts, ext, chip, w, diag, keep, base)

    ext, chip, link = exchange(by_row, (place, shifts, anchor))
    part = near(by_row, ext, chip, (True, False))
    force = call(far_first_body, f32(*part.shape), [SMEM] * 3 + [VMEM] * 4)(
        place, shifts, anchor, part, link, w, keep
    )
    ext, chip, link = exchange(force)
    part = near(force, ext, chip, (False, False))
    second = call(far_body, f32(*part.shape), [SMEM] * 2 + [VMEM] * 3)(place, shifts, part, link, w)
    ext, chip, link = exchange(second[:1])
    third, early = call(
        near_last_body, [f32(*second[:1].shape), f32(1, 128)], [SMEM] * 2 + [VMEM] * 9
    )(place, shifts, ext, chip, w, diag, keep, base, by_row, force, second)
    third, part = call(
        far_last_body, [f32(*third.shape), f32(devices, 1, 128)], [SMEM] * 2 + [VMEM] * 7
    )(place, shifts, third, link, w, early, by_row, force, second)

    parts = lax.all_to_all(part, SEC_TILE, 0, 0, tiled=True)
    coef = call(solve_body, f32(1, 128), [VMEM])(parts)[0]

    def measured(coef):
        basis = (by_row[1], force[0], force[1], second[0], second[1], third[0])

        def norms(x):
            vec = sum(a * b for a, b in zip(x, basis))
            return lax.psum(jnp.sum(vec * vec), SEC_TILE)

        vel, move, _ = coefficients({(0, 0): coef[0] * 0.0}, norms)
        return jnp.concatenate([jnp.stack(vel + move), coef[2 * NB :]])

    coef = lax.cond(coef[2 * NB] > 0.5, measured, lambda coef: coef, coef)

    flat = lambda x: x.reshape(*x.shape[:3], height * q, 128)
    return call(
        final_body,
        [f32(*displacement.shape)] * 2,
        [SMEM] + [VMEM] * 4,
        scratch=[pltpu.VMEM((2, height * q, 128), jnp.float32)],
    )(coef, start, flat(force), flat(second), flat(third))


def solution(mesh):
    torus = Mesh(
        mesh.devices.reshape(2, 4, 2, 2, 8), ("sec_0", "sec_1", "sec_2", "tile_0", "tile_1")
    )
    in_specs = (
        P(None, SEC, TILE, None),
        P(None, SEC, TILE, None),
        P(None, None, SEC, TILE, None),
        P(None, SEC, TILE, None),
        P(SEC, TILE, None),
        P(SEC, None),
    )
    out_specs = (P(None, SEC, TILE, None), P(None, SEC, TILE, None))
    return jax.shard_map(
        shards, mesh=torus, in_specs=in_specs, out_specs=out_specs, check_vma=False
    )
```

```python
import jax
import jax.numpy as jnp
from jax import lax
from jax.experimental import pallas as pl
from jax.experimental.pallas import tpu as pltpu
from jax.sharding import Mesh
from jax.sharding import PartitionSpec as P


ITERS = 3
SEC = ("sec_0", "sec_1", "sec_2")
TILE = ("tile_0", "tile_1")
SEC_TILE = SEC + TILE

in_stiff = 1.0
anchor_stiff = 0.25
cross_stiff = (0.25, 0.5, 0.5, 0.25)
reaches = (-2, -1, 1, 2)
ALPHAS = tuple(0.1 * 0.99**k for k in range(ITERS))
DELTAS = tuple(0.25 * 1.1**k for k in range(ITERS))
UP, DOWN = 2, 3
TINY = 1e-06
NB = 6
PAIRS = [(i, j) for i in range(NB) for j in range(i, NB)]
CANCEL = 1000.0

VMEM = pl.BlockSpec(memory_space=pltpu.VMEM)
SMEM = pl.BlockSpec(memory_space=pltpu.SMEM)
HBM = pl.BlockSpec(memory_space=pltpu.HBM)


def call(body, out_shape, in_specs, flops=4_000_000, bytes_accessed=4_000_000, scratch=(), vmem=16 << 20, out=VMEM):
    multi = isinstance(out_shape, (list, tuple))
    return pl.pallas_call(
        body,
        out_shape=out_shape,
        in_specs=in_specs,
        out_specs=[out] * len(out_shape) if multi else out,
        scratch_shapes=list(scratch),
        compiler_params=pltpu.CompilerParams(vmem_limit_bytes=vmem),
        cost_estimate=pl.CostEstimate(flops=flops, bytes_accessed=bytes_accessed, transcendentals=0),
    )


def f32(*shape):
    return jax.ShapeDtypeStruct(shape, jnp.float32)


def relayout(u_ref, out_ref):
    comps, count, height, width = u_ref.shape
    q = width // 128
    for s in range(count):
        for j in range(q):
            for c in range(comps):
                rows = pl.ds(j, height, stride=q)
                out_ref.at[0, c, s][rows, :] = u_ref[c, s, :, pl.ds(128 * j, 128)]


def relayout_moving(vel_ref, fixed_ref, out_ref):
    comps, count, height, width = vel_ref.shape
    q = width // 128
    for s in range(count):
        for j in range(q):
            cols = pl.ds(128 * j, 128)
            keep = (1 - fixed_ref[s, :, cols]).astype(jnp.float32)
            for c in range(comps):
                rows = pl.ds(j, height, stride=q)
                out_ref.at[0, c, s][rows, :] = vel_ref[c, s, :, cols] * keep


def weights(
    place_ref, offsets_ref, frac_ref, fixed_ref,
    w_ref, diag_ref, keep_ref, base_ref, frac,
):
    count, height, width = fixed_ref.shape
    q = width // 128
    sec_first, row_first, sections, rows = (place_ref[k] for k in range(4))
    for s in range(count):
        for j in range(q):
            cols = pl.ds(128 * j, 128)
            at = pl.ds(j, height, stride=q)
            keep_ref.at[s][at, :] = (1 - fixed_ref[s, :, cols]).astype(jnp.float32)
            for i in range(4):
                for c in range(2):
                    frac.at[c, i][at, :] = frac_ref[c, i, s, :, cols].astype(jnp.float32)
        sub = lax.broadcasted_iota(jnp.int32, (q, 128), 0)
        gcol = lax.broadcasted_iota(jnp.int32, (q, 128), 1) + 128 * sub
        col_links = (gcol > 0).astype(jnp.float32) + (gcol < width - 1).astype(jnp.float32)
        springs = []
        for i in range(4):
            dr, dc = offsets_ref[s, 0, i], offsets_ref[s, 1, i]
            other = sec_first + s + reaches[i]
            there = (other >= 0) & (other < sections)
            col_ok = (gcol + dc >= 0) & (gcol + dc + 1 <= width - 1) & there
            springs.append((dr, dc, jnp.where(col_ok, cross_stiff[i], 0.0)))
        for r in range(height):
            at = pl.ds(r * q, q)
            grow = row_first + r
            row_links = jnp.where(grow > 0, 1.0, 0.0) + jnp.where(grow < rows - 1, 1.0, 0.0)
            keep = keep_ref[s, at, :]
            total = keep * (in_stiff * (row_links + col_links) + anchor_stiff)
            base = [jnp.zeros((q, 128), jnp.float32) for _ in range(2)]
            for i in range(4):
                dr, dc, col_stiff = springs[i]
                row_ok = (grow + dr >= 0) & (grow + dr + 1 <= rows - 1)
                stiff = col_stiff * keep * jnp.where(row_ok, 1.0, 0.0)
                frow, fcol = frac[0, i, at, :], frac[1, i, at, :]
                low = stiff * frow
                high = stiff - low
                w11 = low * fcol
                w01 = high * fcol
                w_ref[s, i, 0, at, :] = high - w01
                w_ref[s, i, 1, at, :] = w01
                w_ref[s, i, 2, at, :] = low - w11
                w_ref[s, i, 3, at, :] = w11
                total = total + stiff
                base[0] = base[0] + stiff * (dr.astype(jnp.float32) + frow)
                base[1] = base[1] + stiff * (dc.astype(jnp.float32) + fcol)
            diag_ref[s, at, :] = total
            for c in range(2):
                base_ref[c, s, at, :] = base[c]


def stay(ext, diag, keep, base, out, affine):
    vecs, comps, count, tall, q, lanes = ext.shape
    height = tall - UP - DOWN
    lane = lax.broadcasted_iota(jnp.int32, (q, lanes), 1)
    sub = lax.broadcasted_iota(jnp.int32, (q, lanes), 0)
    first = (sub == 0) & (lane == 0)
    last = (sub == q - 1) & (lane == lanes - 1)
    for s in range(count):
        for r in range(height):
            at = pl.ds(r * q, q)
            kept, own = keep[s, at, :], diag[s, at, :]
            for v in range(vecs):
                for c in range(comps):
                    x = ext[v, c, s, r + UP]
                    before = jnp.where(lane < lanes - 1, x, pltpu.roll(x, 1, 0))
                    after = jnp.where(lane >= 1, x, pltpu.roll(x, q - 1, 0))
                    before = jnp.where(first, 0.0, pltpu.roll(before, 1, 1))
                    after = jnp.where(last, 0.0, pltpu.roll(after, lanes - 1, 1))
                    near = in_stiff * (ext[v, c, s, r + UP - 1] + ext[v, c, s, r + UP + 1] + before + after)
                    y = kept * near - own * x
                    if affine[v]:
                        y = y + base[c, s, at, :]
                    out[v, c, s, r] = y


def pull(offsets_ref, source, index, s, i, w, out):
    vecs, comps, _, tall, q, lanes = source.shape
    height = tall - UP - DOWN
    lane = lax.broadcasted_iota(jnp.int32, (q, lanes), 1)
    dr, dc = offsets_ref[s, 0, i], offsets_ref[s, 1, i]
    ahead = dc >= 0
    turn = jnp.where(ahead, q - 1, 1)
    shift0 = lax.rem(lanes - dc, lanes)
    shift1 = lax.rem(lanes - dc - 1, lanes)
    low0 = jnp.where(ahead, dc, 0)
    high0 = jnp.where(ahead, lanes, lanes + dc)
    low1 = jnp.where(ahead, dc + 1, 0)
    high1 = jnp.where(ahead, lanes, lanes + dc + 1)
    own0 = (lane >= low0) & (lane < high0)
    own1 = (lane >= low1) & (lane < high1)
    held = {}
    for k in range(height + 1):
        if k > 0:
            at = pl.ds((k - 1) * q, q)
            w00, w01, w10, w11 = (w[s, i, n, at, :] for n in range(4))
        for v in range(vecs):
            for c in range(comps):
                x = source[v, c, index, k + UP + dr]
                y = pltpu.roll(x, turn, 0)
                a0 = pltpu.roll(jnp.where(own0, x, y), shift0, 1)
                a1 = pltpu.roll(jnp.where(own1, x, y), shift1, 1)
                if k > 0:
                    p0, p1 = held[v, c]
                    term = (w00 * p0 + w01 * p1) + (w10 * a0 + w11 * a1)
                    out[v, c, s, k - 1] += term
                held[v, c] = (a0, a1)


def pull_pair(odd, offsets, source, w, out):
    for behind, ahead in (((0, 0, 0), (0, 3, 0)), ((0, 1, 1), (1, 2, 0)), ((1, 0, 1), (1, 3, 1))):
        s, i, index = (jnp.where(odd, b, a) for a, b in zip(behind, ahead))
        pull(offsets, source, index, s, i, w, out)


def near_body(affine, place, offsets, ext, chip, w, diag, keep, base, out):
    stay(ext, diag, keep, base, out, affine)
    pull(offsets, ext, 1, 0, 2, w, out)
    pull(offsets, ext, 0, 1, 1, w, out)
    pull_pair(place[4] == 0, offsets, chip, w, out)


def far_body(place, offsets, part, link, w, out):
    out[...] = part[...]
    pull_pair(place[4] == 1, offsets, link, w, out)


def far_first_body(place, offsets, before, trans, part, link, w, keep, moving, out):
    _, comps, count, height, q, _ = out.shape
    out[1:] = moving[...]
    for s in range(count):
        for c in range(comps):
            anchor = before[c]
            for earlier in range(s + 1):
                anchor = anchor + trans[earlier, c]
            pulled = anchor_stiff * anchor
            for r in range(height):
                out[0, c, s, r] = part[0, c, s, r] + keep[s, pl.ds(r * q, q), :] * pulled
    pull_pair(place[4] == 1, offsets, link, w, out)


def products(pairs, blocks):
    comps, count, height, q, lanes = next(iter(blocks.values()))[0].shape[1:]
    sums = [jnp.zeros((8, lanes), jnp.float32) for _ in pairs]
    for c in range(comps):
        for s in range(count):
            for r in range(height):
                for h in range(q // 8):
                    at = pl.ds(8 * h, 8)
                    vec = {n: ref[v, c, s, r, at, :] for n, (ref, v) in blocks.items()}
                    sums = [g + vec[i] * vec[j] for g, (i, j) in zip(sums, pairs)]
    lane = lax.broadcasted_iota(jnp.int32, (1, lanes), 1)
    packed = jnp.zeros((1, lanes), jnp.float32)
    for pair, g in zip(pairs, sums):
        packed = jnp.where(lane == PAIRS.index(pair), jnp.sum(g), packed)
    return packed


EARLY = [pair for pair in PAIRS if pair[1] < NB - 2]
LATE = [pair for pair in PAIRS if pair[1] >= NB - 2]


def basis(*stages):
    return {2 * k + n: (stage, 1 - n) for k, stage in enumerate(stages) for n in range(2)}


def near_last_body(affine, place, offsets, ext, chip, w, diag, keep, base, force, second, out, early):
    near_body(affine, place, offsets, ext, chip, w, diag, keep, base, out)
    early[...] = products(EARLY, basis(force, second))


def far_last_body(place, offsets, part, link, w, early, force, second, out, sums):
    far_body(place, offsets, part, link, w, out)
    late = products(LATE, basis(force, second, out))
    sums[...] = jnp.broadcast_to((early[...] + late)[None], sums.shape)


def coefficients(gram, norms=None):
    zero = jnp.zeros_like(gram[0, 0])
    one = zero + 1.0
    vel = [one] + [zero] * (NB - 1)
    move = [zero] * NB
    force = [zero, one] + [zero] * (NB - 2)
    bad = zero

    def form(x):
        total, size = zero, zero
        for i, j in PAIRS:
            term = x[i] * x[j] * gram[i, j] * (1.0 if i == j else 2.0)
            total, size = total + term, size + jnp.abs(term)
        return jnp.maximum(total, 0.0), size

    for step in range(ITERS):
        alpha, delta = ALPHAS[step], DELTAS[step]
        if norms is None:
            (ff, fs), (vv, vs) = form(force), form(vel)
            lost = (fs > CANCEL * (ff + TINY)) | (vs > CANCEL * (vv + TINY))
            bad = jnp.where(lost, 1.0, bad)
        else:
            ff, vv = norms(force), norms(vel)
        ratio = jnp.sqrt(vv / (ff + TINY))
        gain = alpha * ratio + delta
        vel = [(1.0 - alpha) * a + gain * f for a, f in zip(vel, force)]
        move = [m + delta * a for m, a in zip(move, vel)]
        force = [zero, one] + move[: NB - 2]
    return vel, move, bad


def solve_body(parts, out, lost):
    lanes = parts.shape[-1]
    total = jnp.sum(parts[...], axis=0)
    lane = lax.broadcasted_iota(jnp.int32, (1, lanes), 1)
    gram = {
        pair: jnp.sum(jnp.where(lane == n, total, 0.0), axis=1, keepdims=True)
        for n, pair in enumerate(PAIRS)
    }
    vel, move, bad = coefficients(gram)
    packed = jnp.zeros((1, lanes), jnp.float32)
    for n, value in enumerate(vel + move):
        packed = jnp.where(lane == n, value, packed)
    out[...] = packed
    lost[...] = (bad > 0.5).astype(jnp.int32)


def final_body(coef, start, force, second, third, u_hbm, v_hbm, flat, rows, sems):
    _, blocks, height, width = rows.shape
    q = width // 128
    vel = [coef[n] for n in range(NB)]
    move = [coef[NB + n] for n in range(NB)]
    order = basis(force, second, third)
    count = start.shape[2]
    copies = []
    for block in range(blocks):
        c, s = divmod(block, count)
        for r in range(height):
            at = pl.ds(r * q, q)
            vec = [ref[n, c, s, at, :] for ref, n in order.values()]
            u = start[0, c, s, at, :]
            v = vel[0] * vec[0]
            u = u + move[0] * vec[0]
            for n in range(1, NB):
                v = v + vel[n] * vec[n]
                u = u + move[n] * vec[n]
            flat[block, 0, at, :] = u
            flat[block, 1, at, :] = v
        for j in range(q):
            at = pl.ds(j, height, stride=q)
            for k in range(2):
                rows[k, block, :, pl.ds(128 * j, 128)] = flat.at[block, k][at, :]
        for k, hbm in enumerate((u_hbm, v_hbm)):
            copies.append(
                pltpu.make_async_copy(rows.at[k, block], hbm.at[c, s], sems.at[k, block])
            )
            copies[-1].start()
    for copy in copies:
        copy.wait()


def swapped(x, axis, first):
    pairs = []
    for i in range(first, lax.axis_size(axis) - 1, 2):
        pairs += [(i, i + 1), (i + 1, i)]
    return lax.ppermute(x, axis, pairs)


def exchange(x, first=()):
    height = x.shape[3]
    odd = lax.axis_index(TILE) % 2 == 1
    edge = lambda top: lax.dynamic_slice_in_dim(x, jnp.where(top, 0, height - DOWN), DOWN, 3)
    outer = swapped(edge(~odd), TILE, 1)
    inner = swapped(edge(odd), TILE, 0)
    link = swapped(lax.optimization_barrier((x, *first))[0] if first else x, SEC, 1)
    above = jnp.where(odd, inner, outer)[:, :, :, DOWN - UP :]
    below = jnp.where(odd, outer, inner)
    edges = jnp.concatenate([above, below], axis=3)
    link_edges = swapped(edges, SEC, 1)
    ext = jnp.concatenate([above, x, below], axis=3)
    chip = swapped(ext, SEC, 0)
    link = jnp.concatenate([link_edges[:, :, :, :UP], link, link_edges[:, :, :, UP:]], axis=3)
    return ext, chip, link


def shards(displacement, velocity, frac, offsets, fixed, trans):
    comps, count, height, width = displacement.shape
    q = width // 128
    devices = lax.axis_size(SEC_TILE)
    place = jnp.stack(
        [
            lax.axis_index(SEC) * count,
            lax.axis_index(TILE) * height,
            jnp.int32(count * lax.axis_size(SEC)),
            jnp.int32(height * lax.axis_size(TILE)),
            lax.axis_index(SEC) % 2,
        ]
    ).astype(jnp.int32)
    shifts = jnp.transpose(offsets[:, :, 0], (1, 2, 0))

    start = call(relayout, f32(1, comps, count, height * q, 128), [VMEM])(displacement)
    by_row = start.reshape(1, comps, count, height, q, 128)
    moving = call(
        relayout_moving, f32(*start.shape), [VMEM] * 2
    )(velocity, fixed).reshape(by_row.shape)

    group = lax.axis_size(SEC)
    moved = jnp.broadcast_to(jnp.sum(trans, 0)[None, None], (group, 1, 2))
    pieces = lax.all_to_all(moved, SEC, 0, 0, tiled=True)
    passed = jnp.arange(group) < lax.axis_index(SEC)
    before = jnp.sum(jnp.where(passed[:, None], pieces[:, 0], 0.0), 0)

    w, diag, keep, base = call(
        weights,
        [
            f32(count, 4, 4, height * q, 128),
            f32(count, height * q, 128),
            f32(count, height * q, 128),
            f32(comps, count, height * q, 128),
        ],
        [SMEM] * 2 + [VMEM] * 2,
        scratch=[pltpu.VMEM((2, 4, height * q, 128), jnp.float32)],
    )(place, shifts, frac, fixed)

    def near(x, ext, chip, affine):
        return call(
            lambda *refs: near_body(affine, *refs), f32(*x.shape), [SMEM] * 2 + [VMEM] * 6
        )(place, shifts, ext, chip, w, diag, keep, base)

    ext, chip, link = exchange(by_row, (place, shifts, before))
    part = near(by_row, ext, chip, (True,))
    both = f32(2, *part.shape[1:])
    force = call(far_first_body, both, [SMEM] * 4 + [VMEM] * 5)(
        place, shifts, before, trans, part, link, w, keep, moving
    )
    ext, chip, link = exchange(force)
    part = near(force, ext, chip, (False, False))
    second = call(far_body, both, [SMEM] * 2 + [VMEM] * 3)(place, shifts, part, link, w)
    ext, chip, link = exchange(second)
    third, early = call(
        lambda *refs: near_last_body((False, False), *refs),
        [both, f32(1, 128)],
        [SMEM] * 2 + [VMEM] * 8,
    )(place, shifts, ext, chip, w, diag, keep, base, force, second)
    third, part = call(
        far_last_body, [both, f32(devices, 1, 128)], [SMEM] * 2 + [VMEM] * 6
    )(place, shifts, third, link, w, early, force, second)

    parts = lax.all_to_all(part, SEC_TILE, 0, 0, tiled=True)
    coef, lost = call(
        solve_body, [f32(1, 128), jax.ShapeDtypeStruct((1, 1), jnp.int32)], [VMEM]
    )(parts)
    coef = coef[0]

    def measured(coef):
        stages = (force, second, third)
        order = [stage[n] for stage in stages for n in (1, 0)]

        def norms(x):
            vec = sum(a * b for a, b in zip(x, order))
            return lax.psum(jnp.sum(vec * vec), SEC_TILE)

        vel, move, _ = coefficients({(0, 0): coef[0] * 0.0}, norms)
        return jnp.concatenate([jnp.stack(vel + move), coef[2 * NB :]])

    coef = lax.cond(lost[0, 0] > 0, measured, lambda coef: coef, coef)

    flat = lambda x: x.reshape(*x.shape[:3], height * q, 128)
    blocks = comps * count
    return call(
        final_body,
        [f32(*displacement.shape)] * 2,
        [SMEM] + [VMEM] * 4,
        scratch=[
            pltpu.VMEM((blocks, 2, height * q, 128), jnp.float32),
            pltpu.VMEM((2, blocks, height, width), jnp.float32),
            pltpu.SemaphoreType.DMA((2, blocks)),
        ],
        out=HBM,
    )(coef, start, flat(force), flat(second), flat(third))


def solution(mesh):
    torus = Mesh(
        mesh.devices.reshape(2, 4, 2, 2, 8), ("sec_0", "sec_1", "sec_2", "tile_0", "tile_1")
    )
    in_specs = (
        P(None, SEC, TILE, None),
        P(None, SEC, TILE, None),
        P(None, None, SEC, TILE, None),
        P(None, SEC, TILE, None),
        P(SEC, TILE, None),
        P(SEC, None),
    )
    out_specs = (P(None, SEC, TILE, None), P(None, SEC, TILE, None))
    return jax.shard_map(
        shards, mesh=torus, in_specs=in_specs, out_specs=out_specs, check_vma=False
    )
```

```python
import jax
import jax.numpy as jnp
from jax import lax
from jax.experimental import pallas as pl
from jax.experimental.pallas import tpu as pltpu
from jax.sharding import Mesh
from jax.sharding import PartitionSpec as P


ITERS = 3
SEC = ("sec_0", "sec_1", "sec_2")
TILE = ("tile_0", "tile_1")
SEC_TILE = SEC + TILE

in_stiff = 1.0
anchor_stiff = 0.25
cross_stiff = (0.25, 0.5, 0.5, 0.25)
reaches = (-2, -1, 1, 2)
ALPHAS = tuple(0.1 * 0.99**k for k in range(ITERS))
DELTAS = tuple(0.25 * 1.1**k for k in range(ITERS))
UP, DOWN = 2, 3
TINY = 1e-06
NB = 6
PAIRS = [(i, j) for i in range(NB) for j in range(i, NB)]
CANCEL = 1000.0

VMEM = pl.BlockSpec(memory_space=pltpu.VMEM)
SMEM = pl.BlockSpec(memory_space=pltpu.SMEM)
HBM = pl.BlockSpec(memory_space=pltpu.HBM)


def call(body, out_shape, in_specs, flops=4_000_000, bytes_accessed=4_000_000, scratch=(), vmem=16 << 20, out=VMEM):
    multi = isinstance(out_shape, (list, tuple))
    return pl.pallas_call(
        body,
        out_shape=out_shape,
        in_specs=in_specs,
        out_specs=[out] * len(out_shape) if multi else out,
        scratch_shapes=list(scratch),
        compiler_params=pltpu.CompilerParams(vmem_limit_bytes=vmem),
        cost_estimate=pl.CostEstimate(flops=flops, bytes_accessed=bytes_accessed, transcendentals=0),
    )


def f32(*shape):
    return jax.ShapeDtypeStruct(shape, jnp.float32)


def relayout(trans_ref, u_ref, out_ref, moved_ref):
    comps, count, height, width = u_ref.shape
    comp = lax.broadcasted_iota(jnp.int32, moved_ref.shape, 2)
    moved = []
    for c in range(comps):
        total = trans_ref[0, c]
        for s in range(1, count):
            total = total + trans_ref[s, c]
        moved.append(total)
    moved_ref[...] = jnp.where(comp == 0, moved[0], moved[1])
    q = width // 128
    for s in range(count):
        for j in range(q):
            for c in range(comps):
                rows = pl.ds(j, height, stride=q)
                out_ref.at[0, c, s][rows, :] = u_ref[c, s, :, pl.ds(128 * j, 128)]


def relayout_moving(vel_ref, fixed_ref, out_ref):
    comps, count, height, width = vel_ref.shape
    q = width // 128
    for s in range(count):
        for j in range(q):
            cols = pl.ds(128 * j, 128)
            keep = (1 - fixed_ref[s, :, cols]).astype(jnp.float32)
            for c in range(comps):
                rows = pl.ds(j, height, stride=q)
                out_ref.at[0, c, s][rows, :] = vel_ref[c, s, :, cols] * keep


def weights(
    place_ref, offsets_ref, frac_ref, fixed_ref,
    w_ref, diag_ref, keep_ref, base_ref, frac,
):
    count, height, width = fixed_ref.shape
    q = width // 128
    sec_first, row_first, sections, rows = (place_ref[k] for k in range(4))
    for s in range(count):
        for j in range(q):
            cols = pl.ds(128 * j, 128)
            at = pl.ds(j, height, stride=q)
            keep_ref.at[s][at, :] = (1 - fixed_ref[s, :, cols]).astype(jnp.float32)
            for i in range(4):
                for c in range(2):
                    frac.at[c, i][at, :] = frac_ref[c, i, s, :, cols].astype(jnp.float32)
        sub = lax.broadcasted_iota(jnp.int32, (q, 128), 0)
        gcol = lax.broadcasted_iota(jnp.int32, (q, 128), 1) + 128 * sub
        col_links = (gcol > 0).astype(jnp.float32) + (gcol < width - 1).astype(jnp.float32)
        springs = []
        for i in range(4):
            dr, dc = offsets_ref[s, 0, i], offsets_ref[s, 1, i]
            other = sec_first + s + reaches[i]
            there = (other >= 0) & (other < sections)
            col_ok = (gcol + dc >= 0) & (gcol + dc + 1 <= width - 1) & there
            springs.append((dr, dc, jnp.where(col_ok, cross_stiff[i], 0.0)))
        for r in range(height):
            at = pl.ds(r * q, q)
            grow = row_first + r
            row_links = jnp.where(grow > 0, 1.0, 0.0) + jnp.where(grow < rows - 1, 1.0, 0.0)
            keep = keep_ref[s, at, :]
            total = keep * (in_stiff * (row_links + col_links) + anchor_stiff)
            base = [jnp.zeros((q, 128), jnp.float32) for _ in range(2)]
            for i in range(4):
                dr, dc, col_stiff = springs[i]
                row_ok = (grow + dr >= 0) & (grow + dr + 1 <= rows - 1)
                stiff = col_stiff * keep * jnp.where(row_ok, 1.0, 0.0)
                frow, fcol = frac[0, i, at, :], frac[1, i, at, :]
                low = stiff * frow
                high = stiff - low
                w11 = low * fcol
                w01 = high * fcol
                w_ref[s, i, 0, at, :] = high - w01
                w_ref[s, i, 1, at, :] = w01
                w_ref[s, i, 2, at, :] = low - w11
                w_ref[s, i, 3, at, :] = w11
                total = total + stiff
                base[0] = base[0] + stiff * (dr.astype(jnp.float32) + frow)
                base[1] = base[1] + stiff * (dc.astype(jnp.float32) + fcol)
            diag_ref[s, at, :] = total
            for c in range(2):
                base_ref[c, s, at, :] = base[c]


def stay(ext, diag, keep, base, out, affine):
    vecs, comps, count, tall, q, lanes = ext.shape
    height = tall - UP - DOWN
    lane = lax.broadcasted_iota(jnp.int32, (q, lanes), 1)
    sub = lax.broadcasted_iota(jnp.int32, (q, lanes), 0)
    first = (sub == 0) & (lane == 0)
    last = (sub == q - 1) & (lane == lanes - 1)
    for s in range(count):
        for r in range(height):
            at = pl.ds(r * q, q)
            kept, own = keep[s, at, :], diag[s, at, :]
            for v in range(vecs):
                for c in range(comps):
                    x = ext[v, c, s, r + UP]
                    before = jnp.where(lane < lanes - 1, x, pltpu.roll(x, 1, 0))
                    after = jnp.where(lane >= 1, x, pltpu.roll(x, q - 1, 0))
                    before = jnp.where(first, 0.0, pltpu.roll(before, 1, 1))
                    after = jnp.where(last, 0.0, pltpu.roll(after, lanes - 1, 1))
                    near = in_stiff * (ext[v, c, s, r + UP - 1] + ext[v, c, s, r + UP + 1] + before + after)
                    y = kept * near - own * x
                    if affine[v]:
                        y = y + base[c, s, at, :]
                    out[v, c, s, r] = y


def pull(offsets_ref, source, index, s, i, w, out):
    vecs, comps, _, tall, q, lanes = source.shape
    height = tall - UP - DOWN
    lane = lax.broadcasted_iota(jnp.int32, (q, lanes), 1)
    dr, dc = offsets_ref[s, 0, i], offsets_ref[s, 1, i]
    ahead = dc >= 0
    turn = jnp.where(ahead, q - 1, 1)
    shift0 = lax.rem(lanes - dc, lanes)
    shift1 = lax.rem(lanes - dc - 1, lanes)
    low0 = jnp.where(ahead, dc, 0)
    high0 = jnp.where(ahead, lanes, lanes + dc)
    low1 = jnp.where(ahead, dc + 1, 0)
    high1 = jnp.where(ahead, lanes, lanes + dc + 1)
    own0 = (lane >= low0) & (lane < high0)
    own1 = (lane >= low1) & (lane < high1)
    held = {}
    for k in range(height + 1):
        if k > 0:
            at = pl.ds((k - 1) * q, q)
            w00, w01, w10, w11 = (w[s, i, n, at, :] for n in range(4))
        for v in range(vecs):
            for c in range(comps):
                x = source[v, c, index, k + UP + dr]
                y = pltpu.roll(x, turn, 0)
                a0 = pltpu.roll(jnp.where(own0, x, y), shift0, 1)
                a1 = pltpu.roll(jnp.where(own1, x, y), shift1, 1)
                if k > 0:
                    p0, p1 = held[v, c]
                    term = (w00 * p0 + w01 * p1) + (w10 * a0 + w11 * a1)
                    out[v, c, s, k - 1] += term
                held[v, c] = (a0, a1)


def pull_pair(odd, offsets, source, w, out):
    for behind, ahead in (((0, 0, 0), (0, 3, 0)), ((0, 1, 1), (1, 2, 0)), ((1, 0, 1), (1, 3, 1))):
        s, i, index = (jnp.where(odd, b, a) for a, b in zip(behind, ahead))
        pull(offsets, source, index, s, i, w, out)


def near_body(affine, place, offsets, ext, chip, w, diag, keep, base, out):
    stay(ext, diag, keep, base, out, affine)
    pull(offsets, ext, 1, 0, 2, w, out)
    pull(offsets, ext, 0, 1, 1, w, out)
    pull_pair(place[4] == 0, offsets, chip, w, out)


def far_body(place, offsets, part, link, w, out):
    out[...] = part[...]
    pull_pair(place[4] == 1, offsets, link, w, out)


def far_first_body(place, offsets, before, trans, part, link, w, keep, moving, out):
    _, comps, count, height, q, _ = out.shape
    out[1:] = moving[...]
    for s in range(count):
        for c in range(comps):
            anchor = before[c]
            for earlier in range(s + 1):
                anchor = anchor + trans[earlier, c]
            pulled = anchor_stiff * anchor
            for r in range(height):
                out[0, c, s, r] = part[0, c, s, r] + keep[s, pl.ds(r * q, q), :] * pulled
    pull_pair(place[4] == 1, offsets, link, w, out)


def products(pairs, blocks):
    comps, count, height, q, lanes = next(iter(blocks.values()))[0].shape[1:]
    sums = [jnp.zeros((8, lanes), jnp.float32) for _ in pairs]
    for c in range(comps):
        for s in range(count):
            for r in range(height):
                for h in range(q // 8):
                    at = pl.ds(8 * h, 8)
                    vec = {n: ref[v, c, s, r, at, :] for n, (ref, v) in blocks.items()}
                    sums = [g + vec[i] * vec[j] for g, (i, j) in zip(sums, pairs)]
    lane = lax.broadcasted_iota(jnp.int32, (1, lanes), 1)
    packed = jnp.zeros((1, lanes), jnp.float32)
    for pair, g in zip(pairs, sums):
        packed = jnp.where(lane == PAIRS.index(pair), jnp.sum(g), packed)
    return packed


EARLY = [pair for pair in PAIRS if pair[1] < NB - 2]
LATE = [pair for pair in PAIRS if pair[1] >= NB - 2]


def basis(*stages):
    return {2 * k + n: (stage, 1 - n) for k, stage in enumerate(stages) for n in range(2)}


def near_last_body(affine, place, offsets, ext, chip, w, diag, keep, base, force, second, out, early):
    near_body(affine, place, offsets, ext, chip, w, diag, keep, base, out)
    early[...] = products(EARLY, basis(force, second))


def far_last_body(place, offsets, part, link, w, early, force, second, out, sums):
    far_body(place, offsets, part, link, w, out)
    late = products(LATE, basis(force, second, out))
    sums[...] = jnp.broadcast_to((early[...] + late)[None], sums.shape)


def coefficients(gram, norms=None):
    zero = jnp.zeros_like(gram[0, 0])
    one = zero + 1.0
    vel = [one] + [zero] * (NB - 1)
    move = [zero] * NB
    force = [zero, one] + [zero] * (NB - 2)
    bad = zero

    def form(x):
        total, size = zero, zero
        for i, j in PAIRS:
            term = x[i] * x[j] * gram[i, j] * (1.0 if i == j else 2.0)
            total, size = total + term, size + jnp.abs(term)
        return jnp.maximum(total, 0.0), size

    for step in range(ITERS):
        alpha, delta = ALPHAS[step], DELTAS[step]
        if norms is None:
            (ff, fs), (vv, vs) = form(force), form(vel)
            lost = (fs > CANCEL * (ff + TINY)) | (vs > CANCEL * (vv + TINY))
            bad = jnp.where(lost, 1.0, bad)
        else:
            ff, vv = norms(force), norms(vel)
        ratio = jnp.sqrt(vv / (ff + TINY))
        gain = alpha * ratio + delta
        vel = [(1.0 - alpha) * a + gain * f for a, f in zip(vel, force)]
        move = [m + delta * a for m, a in zip(move, vel)]
        force = [zero, one] + move[: NB - 2]
    return vel, move, bad


def solve_body(parts, out, lost):
    lanes = parts.shape[-1]
    total = jnp.sum(jnp.sum(parts[...], axis=0), axis=0, keepdims=True)
    lane = lax.broadcasted_iota(jnp.int32, (1, lanes), 1)
    gram = {
        pair: jnp.sum(jnp.where(lane == n, total, 0.0), axis=1, keepdims=True)
        for n, pair in enumerate(PAIRS)
    }
    vel, move, bad = coefficients(gram)
    packed = jnp.zeros((1, lanes), jnp.float32)
    for n, value in enumerate(vel + move):
        packed = jnp.where(lane == n, value, packed)
    out[...] = packed
    lost[...] = (bad > 0.5).astype(jnp.int32)


def final_body(coef, start, force, second, third, u_hbm, v_hbm, flat, rows, sems):
    _, blocks, height, width = rows.shape
    q = width // 128
    vel = [coef[n] for n in range(NB)]
    move = [coef[NB + n] for n in range(NB)]
    order = basis(force, second, third)
    count = start.shape[2]
    copies = []
    for block in range(blocks):
        c, s = divmod(block, count)
        for r in range(height):
            at = pl.ds(r * q, q)
            vec = [ref[n, c, s, at, :] for ref, n in order.values()]
            u = start[0, c, s, at, :]
            v = vel[0] * vec[0]
            u = u + move[0] * vec[0]
            for n in range(1, NB):
                v = v + vel[n] * vec[n]
                u = u + move[n] * vec[n]
            flat[block, 0, at, :] = u
            flat[block, 1, at, :] = v
        for j in range(q):
            at = pl.ds(j, height, stride=q)
            for k in range(2):
                rows[k, block, :, pl.ds(128 * j, 128)] = flat.at[block, k][at, :]
        for k, hbm in enumerate((u_hbm, v_hbm)):
            copies.append(
                pltpu.make_async_copy(rows.at[k, block], hbm.at[c, s], sems.at[k, block])
            )
            copies[-1].start()
    for copy in copies:
        copy.wait()


def swapped(x, axis, first):
    pairs = []
    for i in range(first, lax.axis_size(axis) - 1, 2):
        pairs += [(i, i + 1), (i + 1, i)]
    return lax.ppermute(x, axis, pairs)


def exchange(x, first=()):
    height = x.shape[3]
    odd = lax.axis_index(TILE) % 2 == 1
    edge = lambda top: lax.dynamic_slice_in_dim(x, jnp.where(top, 0, height - DOWN), DOWN, 3)
    outer = swapped(edge(~odd), TILE, 1)
    inner = swapped(edge(odd), TILE, 0)
    link = swapped(lax.optimization_barrier((x, *first))[0] if first else x, SEC, 1)
    above = jnp.where(odd, inner, outer)[:, :, :, DOWN - UP :]
    below = jnp.where(odd, outer, inner)
    edges = jnp.concatenate([above, below], axis=3)
    link_edges = swapped(edges, SEC, 1)
    ext = jnp.concatenate([above, x, below], axis=3)
    chip = swapped(ext, SEC, 0)
    link = jnp.concatenate([link_edges[:, :, :, :UP], link, link_edges[:, :, :, UP:]], axis=3)
    return ext, chip, link


def shards(displacement, velocity, frac, offsets, fixed, trans):
    comps, count, height, width = displacement.shape
    q = width // 128
    devices = lax.axis_size(SEC_TILE)
    place = jnp.stack(
        [
            lax.axis_index(SEC) * count,
            lax.axis_index(TILE) * height,
            jnp.int32(count * lax.axis_size(SEC)),
            jnp.int32(height * lax.axis_size(TILE)),
            lax.axis_index(SEC) % 2,
        ]
    ).astype(jnp.int32)
    shifts = jnp.transpose(offsets[:, :, 0], (1, 2, 0))

    group = lax.axis_size(SEC)
    start, moved = call(
        relayout, [f32(1, comps, count, height * q, 128), f32(group, 1, comps)], [SMEM, VMEM]
    )(trans, displacement)
    by_row = start.reshape(1, comps, count, height, q, 128)
    moving = call(
        relayout_moving, f32(*start.shape), [VMEM] * 2
    )(velocity, fixed).reshape(by_row.shape)

    pieces = lax.all_to_all(moved, SEC, 0, 0, tiled=True)
    passed = jnp.arange(group) < lax.axis_index(SEC)
    before = jnp.sum(jnp.where(passed[:, None], pieces[:, 0], 0.0), 0)

    w, diag, keep, base = call(
        weights,
        [
            f32(count, 4, 4, height * q, 128),
            f32(count, height * q, 128),
            f32(count, height * q, 128),
            f32(comps, count, height * q, 128),
        ],
        [SMEM] * 2 + [VMEM] * 2,
        scratch=[pltpu.VMEM((2, 4, height * q, 128), jnp.float32)],
    )(place, shifts, frac, fixed)

    def near(x, ext, chip, affine):
        return call(
            lambda *refs: near_body(affine, *refs), f32(*x.shape), [SMEM] * 2 + [VMEM] * 6
        )(place, shifts, ext, chip, w, diag, keep, base)

    ext, chip, link = exchange(by_row, (place, shifts, before))
    part = near(by_row, ext, chip, (True,))
    both = f32(2, *part.shape[1:])
    force = call(far_first_body, both, [SMEM] * 4 + [VMEM] * 5)(
        place, shifts, before, trans, part, link, w, keep, moving
    )
    ext, chip, link = exchange(force)
    part = near(force, ext, chip, (False, False))
    second = call(far_body, both, [SMEM] * 2 + [VMEM] * 3)(place, shifts, part, link, w)
    ext, chip, link = exchange(second)
    third, early = call(
        lambda *refs: near_last_body((False, False), *refs),
        [both, f32(1, 128)],
        [SMEM] * 2 + [VMEM] * 8,
    )(place, shifts, ext, chip, w, diag, keep, base, force, second)
    third, part = call(
        far_last_body, [both, f32(devices // 8, 8, 128)], [SMEM] * 2 + [VMEM] * 6
    )(place, shifts, third, link, w, early, force, second)

    parts = lax.all_to_all(part.reshape(devices, 1, 128), SEC_TILE, 0, 0, tiled=True)
    coef, lost = call(
        solve_body, [f32(1, 128), jax.ShapeDtypeStruct((1, 1), jnp.int32)], [VMEM]
    )(parts.reshape(part.shape))
    coef = coef[0]

    def measured(coef):
        stages = (force, second, third)
        order = [stage[n] for stage in stages for n in (1, 0)]

        def norms(x):
            vec = sum(a * b for a, b in zip(x, order))
            return lax.psum(jnp.sum(vec * vec), SEC_TILE)

        vel, move, _ = coefficients({(0, 0): coef[0] * 0.0}, norms)
        return jnp.concatenate([jnp.stack(vel + move), coef[2 * NB :]])

    coef = lax.cond(lost[0, 0] > 0, measured, lambda coef: coef, coef)

    flat = lambda x: x.reshape(*x.shape[:3], height * q, 128)
    blocks = comps * count
    return call(
        final_body,
        [f32(*displacement.shape)] * 2,
        [SMEM] + [VMEM] * 4,
        scratch=[
            pltpu.VMEM((blocks, 2, height * q, 128), jnp.float32),
            pltpu.VMEM((2, blocks, height, width), jnp.float32),
            pltpu.SemaphoreType.DMA((2, blocks)),
        ],
        out=HBM,
    )(coef, start, flat(force), flat(second), flat(third))


def solution(mesh):
    torus = Mesh(
        mesh.devices.reshape(2, 4, 2, 2, 8), ("sec_0", "sec_1", "sec_2", "tile_0", "tile_1")
    )
    in_specs = (
        P(None, SEC, TILE, None),
        P(None, SEC, TILE, None),
        P(None, None, SEC, TILE, None),
        P(None, SEC, TILE, None),
        P(SEC, TILE, None),
        P(SEC, None),
    )
    out_specs = (P(None, SEC, TILE, None), P(None, SEC, TILE, None))
    return jax.shard_map(
        shards, mesh=torus, in_specs=in_specs, out_specs=out_specs, check_vma=False
    )
```
